512 devices in a mesh: section: 16 (over y, z_lo), expert: 32 (over x, z_hi, core).
Axes of the slice: x: 4, y: 4, z: 16 (z_hi: 4, z_lo: 4; z = z_hi * 4 + z_lo), core: 2. Of those that a mesh axis runs over, the one named last changes fastest.
Arguments:
- grad_out: bfloat16 [16, 2048, 2048], P('section', 'expert'), may hold values from -3 to 3
- pre_act: bfloat16 [16, 2048, 2, 2, 768], P('section', 'expert'), may hold values from -5 to 5
- route_ids: int32 [16, 2048, 2], P('section', 'expert'), may hold values from 0 to 7, as said below
- route_gate: bfloat16 [16, 2048, 2], P('section', 'expert'), may hold values from 0.19921875 to 1
- w_gate: bfloat16 [16, 2048, 6144], P('section', None, 'expert'), may hold values from -0.125 to 0.125
- w_up: bfloat16 [16, 2048, 6144], P('section', None, 'expert'), may hold values from -0.125 to 0.125
- w_down: bfloat16 [16, 6144, 2048], P('section', 'expert'), may hold values from -0.21875 to 0.21875
Outputs:
- grad_in: bfloat16 [16, 2048, 2048], P('section', 'expert')
- grad_down: bfloat16 [16, 6144, 2048], P('section', 'expert')
The draws below stay inside these ranges and needn't reach their ends.
Inputs may be any that keep to these rules, and one draw needn't show every extreme that they name: `route_ids`: each row names 2 different experts. In the rows of one device of one section (aligned blocks of 64 tokens) no expert is named by more than 24 rows, and in every block one expert is named by exactly 24 rows.
All inputs are finite; a program needn't handle non-finite values.
Results may differ from the reference program's by a relative error of at most 0.0065.
Values may be sent and summed in bfloat16 or wider, within the bound.
A program may use at most 64 MiB of HBM per device.

```python
import jax
import jax.numpy as jnp
from jax import lax

D = 2048
FF = 768
EXPERTS = 8
TOPK = 2
TOK_DEV = 64
SECTIONS = 16
TOKENS = 2048
CAP = 24
N_EXPERT = 32


def route_block(key, hot_expert):
    key_hot, key_cold, key_flip, key_perm = jax.random.split(key, 4)
    others = EXPERTS - 1
    offset_hot = jax.random.randint(key_hot, (), 0, others)
    offset_cold = jax.random.randint(key_cold, (), 0, others)
    slot_rank = jnp.arange(TOK_DEV)
    in_hot = slot_rank < CAP
    cold_index = slot_rank - CAP
    hot_second = (hot_expert + 1 + (slot_rank + offset_hot) % others) % EXPERTS
    cold_first = (hot_expert + 1 + (2 * cold_index + offset_cold) % others) % EXPERTS
    cold_second = (hot_expert + 1 + (2 * cold_index + 1 + offset_cold) % others) % EXPERTS
    first_pick = jnp.where(in_hot, hot_expert, cold_first)
    second_pick = jnp.where(in_hot, hot_second, cold_second)
    flipped = jax.random.randint(key_flip, (TOK_DEV,), 0, 2)
    forward_pair = jnp.stack([first_pick, second_pick], axis=1)
    reverse_pair = jnp.stack([second_pick, first_pick], axis=1)
    pairs = jnp.where(flipped[:, None] == 1, reverse_pair, forward_pair)
    row_order = jax.random.permutation(key_perm, TOK_DEV)
    return pairs[row_order]


def draw_route_ids(key, part):
    per_section = TOKENS // TOK_DEV
    block_total = SECTIONS * per_section
    key_hot, key_blocks = jax.random.split(jax.random.fold_in(key, 17))
    hot_blocks = jax.random.randint(key_hot, (block_total,), 0, EXPERTS)
    block_keys = jax.random.split(key_blocks, block_total)
    rows_all = jax.vmap(route_block)(block_keys, hot_blocks)
    return rows_all.reshape(SECTIONS, TOKENS, TOPK).astype(jnp.int32)


def block_scale(own_key, extent, cuts, low, largest):
    factor_of = 1.0
    for dim, shards_of in cuts:
        steps = jax.random.uniform(jax.random.fold_in(jax.random.fold_in(own_key, 6), dim), (shards_of,), jnp.float32, low / len(cuts), largest / len(cuts))
        factor_of = factor_of * jnp.repeat(jnp.exp(steps), extent[dim] // shards_of).reshape((-1,) + (1,) * (len(extent) - 1 - dim))
    return factor_of


def scatter_about(own_key, shape, width, bound, cuts=(), held_as=jnp.bfloat16):
    values = jax.random.normal(own_key, shape, jnp.float32) * width
    if len(cuts) > 0:
        values = block_scale(own_key, shape, cuts, -0.22, 0.18) * values
    return jnp.clip(values, min=-bound, max=bound).astype(held_as)


def setup_inputs(seed: int = 0) -> dict:
    key_list = jax.random.split(jax.random.key(seed), 8)
    grad_out = scatter_about(key_list[0], (SECTIONS, TOKENS, D), 0.5, 3.0, ((0, 16), (1, 32)))
    pre_act = scatter_about(key_list[1], (SECTIONS, TOKENS, TOPK, 2, FF), 1.0, 5.0, ((0, 16), (1, 32)))
    route_ids = draw_route_ids(jax.random.fold_in(key_list[7], 71), 0)
    route_gate = jnp.clip(0.19921875 + 0.80078125 * jax.random.uniform(key_list[3], (SECTIONS, TOKENS, TOPK), jnp.float32) ** block_scale(key_list[3], (SECTIONS, TOKENS, TOPK), ((0, 16), (1, 32)), -0.2, 0.2), 0.19921875, 1.0).astype(jnp.bfloat16)
    w_gate = scatter_about(key_list[4], (SECTIONS, D, EXPERTS * FF), D ** -0.5, 0.125, ((0, 16), (2, 32)))
    w_up = scatter_about(key_list[5], (SECTIONS, D, EXPERTS * FF), D ** -0.5, 0.125, ((0, 16), (2, 32)))
    w_down = scatter_about(key_list[6], (SECTIONS, EXPERTS * FF, D), FF ** -0.5, 0.21875, ((0, 16), (1, 32)))
    return dict(grad_out=grad_out, pre_act=pre_act, route_ids=route_ids, route_gate=route_gate, w_gate=w_gate, w_up=w_up, w_down=w_down)


def section_grads(inputs):
    upstream, saved_acts, route_rows, gate_vals, weight_gate, weight_up, weight_down = inputs
    block_total = TOKENS // TOK_DEV
    group_size = N_EXPERT // EXPERTS
    hid_units = FF // group_size
    picked = route_rows[:, :, None] == jnp.arange(EXPERTS, dtype=jnp.int32)[None, None, :]
    is_named = jnp.any(picked, axis=1).reshape(block_total, TOK_DEV, EXPERTS).astype(jnp.int32)
    slot_rank = jnp.cumsum(is_named, axis=1) - 1
    slot_index = jnp.where(is_named > 0, slot_rank, -1)
    upstream_f = upstream.reshape(block_total, TOK_DEV, D).astype(jnp.float32)
    token_grad = jnp.zeros((block_total, TOK_DEV, D), jnp.float32)
    down_parts = []
    high = lax.Precision.HIGHEST
    for expert_no in range(EXPERTS):
        selector = (slot_index[:, :, expert_no][:, None, :] == jnp.arange(CAP, dtype=jnp.int32)[None, :, None]).astype(jnp.float32)
        rows_up = jnp.einsum("bct,btd->bcd", selector, upstream_f, precision=high).reshape(-1, D).astype(jnp.bfloat16)
        gate_sel = jnp.sum(jnp.where(picked[:, :, expert_no], gate_vals.astype(jnp.float32), 0.0), axis=1)
        rows_gate = jnp.einsum("bct,bt->bc", selector, gate_sel.reshape(block_total, TOK_DEV), precision=high).reshape(-1)
        saved_sel = jnp.zeros((TOKENS, 2, FF), jnp.float32)
        for pick_index in range(TOPK):
            saved_sel = jnp.where(picked[:, pick_index, expert_no][:, None, None], saved_acts[:, pick_index].astype(jnp.float32), saved_sel)
        rows_saved = jnp.einsum("bct,btx->bcx", selector, saved_sel.reshape(block_total, TOK_DEV, 2 * FF), precision=high).reshape(-1, 2 * FF)
        gate_pre = rows_saved[:, :FF]
        up_pre = rows_saved[:, FF:]
        low_col = expert_no * FF
        down_block = weight_down[low_col:low_col + FF]
        gate_block = weight_gate[:, low_col:low_col + FF]
        up_block = weight_up[:, low_col:low_col + FF]
        grad_hidden = jnp.dot(rows_up, down_block.T, preferred_element_type=jnp.float32) * rows_gate[:, None]
        sigmoid_g = jax.nn.sigmoid(gate_pre)
        silu_val = gate_pre * sigmoid_g
        grad_gate = (grad_hidden * up_pre * sigmoid_g * (1.0 + gate_pre * (1.0 - sigmoid_g))).astype(jnp.bfloat16)
        grad_upper = (grad_hidden * silu_val).astype(jnp.bfloat16)
        scaled_hidden = (rows_gate[:, None] * silu_val * up_pre).astype(jnp.bfloat16)
        down_parts.append(jnp.dot(scaled_hidden.T, rows_up, preferred_element_type=jnp.float32).astype(jnp.bfloat16))
        summed = jnp.zeros((block_total * CAP, D), jnp.float32)
        for member_no in range(group_size):
            low_unit = member_no * hid_units
            slice_term = jnp.dot(grad_gate[:, low_unit:low_unit + hid_units], gate_block[:, low_unit:low_unit + hid_units].T, preferred_element_type=jnp.float32)
            slice_term = slice_term + jnp.dot(grad_upper[:, low_unit:low_unit + hid_units], up_block[:, low_unit:low_unit + hid_units].T, preferred_element_type=jnp.float32)
            rounded = lax.optimization_barrier(slice_term.astype(jnp.bfloat16))
            summed = summed + rounded.astype(jnp.float32)
        member_total = lax.optimization_barrier(summed.astype(jnp.bfloat16)).astype(jnp.float32)
        token_grad = token_grad + jnp.einsum("bct,bcd->btd", selector, member_total.reshape(block_total, CAP, D), precision=high)
    return token_grad.reshape(TOKENS, D).astype(jnp.bfloat16), jnp.concatenate(down_parts, axis=0)


def reference(grad_out, pre_act, route_ids, route_gate, w_gate, w_up, w_down):
    token_grads, grad_down = lax.map(section_grads, (grad_out, pre_act, route_ids, route_gate, w_gate, w_up, w_down))
    grad_in = jnp.roll(token_grads, -1, axis=0)
    return grad_in, grad_down
```

```python
import jax
import jax.numpy as jnp
from jax import lax
from jax.sharding import PartitionSpec as P

EXPERTS = 8


def on_device(grad_out, pre_act, route_ids, route_gate, w_gate, w_up, w_down):
    members = lax.axis_size("expert")
    group = members // EXPERTS
    tokens = grad_out.shape[1]
    width = grad_out.shape[2]
    hid = w_down.shape[1]
    cap = 3 * tokens // 8
    upstream = grad_out[0]
    route = route_ids[0]
    gates = route_gate[0]
    saved = pre_act[0].reshape(tokens * 2, -1)
    experts = jnp.arange(EXPERTS, dtype=jnp.int32)
    named = jnp.any(route[:, :, None] == experts, axis=1).astype(jnp.int32)
    slot = jnp.where(named > 0, jnp.cumsum(named, axis=0) - 1, -1)
    slot_tk = jnp.where(
        route[:, :, None] == experts, slot[:, None, :], -1
    ).reshape(tokens * 2, EXPERTS)
    pick = slot_tk.T[:, None, :] == jnp.arange(cap, dtype=jnp.int32)[None, :, None]
    rows = jnp.dot(
        pick.astype(jnp.bfloat16).reshape(EXPERTS * cap, tokens * 2),
        saved,
        preferred_element_type=jnp.float32,
    ).astype(jnp.bfloat16)
    rows = rows.reshape(EXPERTS, cap, 2, group, hid).transpose(0, 3, 1, 2, 4)
    rows = rows.reshape(members, cap, 2 * hid)
    recv = lax.all_to_all(rows, "expert", split_axis=0, concat_axis=0, tiled=True)
    all_up = lax.all_gather(upstream, "expert", axis=0, tiled=True)
    all_route = lax.all_gather(route, "expert", axis=0, tiled=True)
    all_gate = lax.all_gather(gates, "expert", axis=0, tiled=True)
    mine = lax.axis_index("expert") // group
    hit = all_route == mine
    gate = jnp.sum(jnp.where(hit, all_gate.astype(jnp.float32), 0.0), axis=1)
    is_mine = jnp.any(hit, axis=1).reshape(members, tokens)
    rank = jnp.where(is_mine, jnp.cumsum(is_mine.astype(jnp.int32), axis=1) - 1, -1)
    expand = (rank[:, :, None] == jnp.arange(cap, dtype=jnp.int32)).astype(jnp.bfloat16)
    acts = jnp.einsum(
        "btc,bcx->btx", expand, recv, preferred_element_type=jnp.float32
    ).reshape(members * tokens, 2 * hid)
    a = acts[:, :hid]
    b = acts[:, hid:]
    weight_down = w_down[0]
    last = (((1,), (1,)), ((), ()))
    grad_h = gate[:, None] * lax.dot_general(
        all_up, weight_down, last, preferred_element_type=jnp.float32
    )
    sig = jax.nn.sigmoid(a)
    silu = a * sig
    grad_a = (grad_h * b * sig * (1.0 + a * (1.0 - sig))).astype(jnp.bfloat16)
    grad_b = (grad_h * silu).astype(jnp.bfloat16)
    scaled = (gate[:, None] * silu * b).astype(jnp.bfloat16)
    back = lax.dot_general(grad_a, w_gate[0], last, preferred_element_type=jnp.float32)
    back = back + lax.dot_general(
        grad_b, w_up[0], last, preferred_element_type=jnp.float32
    )
    grad_down = lax.dot_general(
        scaled, all_up, (((0,), (0,)), ((), ())), preferred_element_type=jnp.float32
    ).astype(jnp.bfloat16)
    total = lax.psum_scatter(
        back.astype(jnp.bfloat16), "expert", scatter_dimension=0, tiled=True
    )
    count = lax.axis_size("section")
    pairs = [(source, (source - 1) % count) for source in range(count)]
    shifted = lax.ppermute(total, "section", pairs)
    return shifted[None], grad_down[None]


def solution(mesh):
    tok = P("section", "expert", None)
    return jax.shard_map(
        on_device,
        mesh=mesh,
        in_specs=(
            tok,
            P("section", "expert", None, None, None),
            tok,
            tok,
            P("section", None, "expert"),
            P("section", None, "expert"),
            tok,
        ),
        out_specs=(tok, tok),
        check_vma=False,
    )
```

```python
import functools

import jax
import jax.numpy as jnp
from jax import lax
from jax.experimental import pallas as pl
from jax.experimental.pallas import tpu as pltpu
from jax.sharding import PartitionSpec as P

EXPERTS = 8
ROWS = 16
MESH = pl.DeviceIdType.MESH
VMEM = pltpu.VMEM


class Wire:
    def __init__(self, send_sems, recv_sems):
        self.send_sems = send_sems
        self.recv_sems = recv_sems
        self.sent = []
        self.used = {}

    def recv_sem(self, key):
        if key not in self.used:
            self.used[key] = len(self.used)
        return self.recv_sems.at[self.used[key]]

    def send(self, src, dst, key, device):
        copy = pltpu.make_async_remote_copy(
            src_ref=src,
            dst_ref=dst,
            send_sem=self.send_sems.at[len(self.sent)],
            recv_sem=self.recv_sem(key),
            device_id=device,
            device_id_type=MESH,
        )
        copy.start()
        self.sent.append(copy)

    def arrive(self, dst, key, device):
        pltpu.make_async_remote_copy(
            src_ref=dst,
            dst_ref=dst,
            send_sem=self.send_sems.at[0],
            recv_sem=self.recv_sem(key),
            device_id=device,
            device_id_type=MESH,
        ).wait_recv()

    def drain(self):
        for copy in self.sent:
            copy.wait_send()


def place():
    me = lax.axis_index("expert")
    x = me // 8
    z = lax.rem(me // 2, 4)
    c = lax.rem(me, 2)

    def dev(dx, dz, dc):
        core = c if dc == 0 else 1 - c
        return {"expert": lax.rem(x + dx, 4) * 8 + lax.rem(z + dz, 4) * 2 + core}

    return x, z, c, dev


def greet(devices):
    barrier = pltpu.get_barrier_semaphore()
    for device in devices:
        pl.semaphore_signal(barrier, inc=1, device_id=device, device_id_type=MESH)
    pl.semaphore_wait(barrier, len(devices))


def dispatch_kernel(
    up_ref, slots_ref, meta_ref, all_up_ref, acts_ref, all_meta_ref,
    up, meta, held, acts, far, send_sems, recv_sems, copy_sems,
):
    x, z, c, dev = place()
    greet(
        [dev(0, 1, 0), dev(0, 3, 0), dev(0, 1, 1), dev(0, 3, 1)]
        + [dev(1, 0, 0), dev(2, 0, 0), dev(3, 0, 0), dev(0, 0, 1)]
    )
    wire = Wire(send_sems, recv_sems)
    here = dev(0, 0, 1)
    chunks = up_ref.shape[0]
    local = []

    def keep(src, dst):
        copy = pltpu.make_async_copy(src, dst, copy_sems.at[len(local)])
        copy.start()
        local.append(copy)
        return copy

    ahead = 1 + 2 * c
    behind = 3 - 2 * c
    core = (c, 1 - c)
    far_z = lax.rem(z + 2, 4)
    for dc in (0, 1):
        step = ahead if dc == 0 else behind
        wire.send(slots_ref.at[:, far_z, core[dc]], far.at[dc], ("far", dc), dev(0, step, dc))
    for step in (1, 3):
        for dc in (0, 1):
            wire.send(
                slots_ref.at[:, lax.rem(z + step, 4), core[dc]],
                held.at[dc, 4 - step],
                ("held", dc, 4 - step),
                dev(0, step, dc),
            )
    wire.send(slots_ref.at[:, z, core[1]], held.at[1, 0], ("held", 1, 0), dev(0, 0, 1))
    own_slots = keep(slots_ref.at[:, z, c], held.at[0, 0])

    def view(q):
        if q < 0:
            return meta_ref, lambda dc, dx, *dz: meta.at[(dc, dx) + dz]
        return up_ref.at[q], lambda dc, dx, *dz: up.at[(q, dc, dx) + dz]

    def stage_a(q):
        mine, at = view(q)
        wire.send(mine, at(0, 0, 3), ("z", q, 3), dev(0, 1, 0))
        wire.send(mine, at(0, 0, 1), ("z", q, 1), dev(0, 3, 0))
        wire.send(mine, at(0, 3, 0), ("x", q, 3, 0), dev(1, 0, 0))
        wire.send(mine, at(0, 1, 0), ("x", q, 1, 0), dev(3, 0, 0))
        keep(mine, at(0, 0, 0))

    def along_x(q, dz):
        _, at = view(q)
        wire.send(at(0, 0, dz), at(0, 3, dz), ("x", q, 3, dz), dev(1, 0, 0))
        wire.send(at(0, 0, dz), at(0, 1, dz), ("x", q, 1, dz), dev(3, 0, 0))

    def stage_b(q):
        _, at = view(q)
        order = (1, 3) if q % 2 == 0 else (3, 1)
        for near in order:
            wire.arrive(at(0, 0, near), ("z", q, near), here)
            if near == order[0]:
                wire.send(at(0, 0, near), at(0, 0, 2), ("z", q, 2), dev(0, 4 - near, 0))
            along_x(q, near)

    def stage_c(q):
        _, at = view(q)
        wire.arrive(at(0, 0, 2), ("z", q, 2), here)
        along_x(q, 2)
        local[1 + q + 1].wait()
        wire.send(at(0, 0), at(1, 0), ("c", q, 0), dev(0, 0, 1))

    def stage_d(q):
        _, at = view(q)
        order = (1, 3) if q % 2 == 0 else (3, 1)
        for near in order:
            for dz in range(4):
                wire.arrive(at(0, near, dz), ("x", q, near, dz), here)
            if near == order[0]:
                wire.send(at(0, near), at(0, 2), ("x", q, 2), dev(4 - near, 0, 0))
            wire.send(at(0, near), at(1, near), ("c", q, near), dev(0, 0, 1))

    def stage_e(q):
        _, at = view(q)
        wire.arrive(at(0, 2), ("x", q, 2), here)
        wire.send(at(0, 2), at(1, 2), ("c", q, 2), dev(0, 0, 1))

    def stage_f(q):
        _, at = view(q)
        for dx in range(4):
            wire.arrive(at(1, dx), ("c", q, dx), here)
        if q >= 0:
            keep(up.at[q], all_up_ref.at[q])

    def slots_far():
        for dc in (0, 1):
            wire.arrive(far.at[dc], ("far", dc), here)
            wire.send(far.at[dc], held.at[dc, 2], ("held", dc, 2), dev(0, ahead, 0))

    def slots_x():
        own_slots.wait()
        for dc in (0, 1):
            for dz in range(4):
                if (dc, dz) != (0, 0):
                    wire.arrive(held.at[dc, dz], ("held", dc, dz), here)
        for dx in (1, 3, 2):
            wire.send(
                held.at[:, :, lax.rem(x + dx, 4)],
                acts.at[:, (4 - dx) % 4],
                ("acts", (4 - dx) % 4),
                dev(dx, 0, 0),
            )

    stage_a(-1)
    for q in range(chunks):
        stage_a(q)
    slots_far()
    stage_b(-1)
    slots_x()
    own_acts = keep(held.at[:, :, x], acts.at[:, 0])
    stage_c(-1)
    for step in range(chunks + 3):
        for lag, stage in enumerate((stage_b, stage_c)):
            q = step - lag
            if 0 <= q < chunks:
                stage(q)
        if step == 0:
            stage_d(-1)
        for lag, stage in enumerate((stage_d, stage_e)):
            q = step - lag - 2
            if 0 <= q < chunks:
                stage(q)
        if step == 1:
            stage_e(-1)
            stage_f(-1)
    own_acts.wait()
    for dx in (1, 3, 2):
        wire.arrive(acts.at[:, dx], ("acts", dx), here)
    outs = [
        pltpu.make_async_copy(acts, acts_ref, copy_sems.at[0]),
        pltpu.make_async_copy(meta, all_meta_ref, copy_sems.at[1]),
    ]
    for copy in outs:
        copy.start()
    done = len(local)
    for q in range(chunks):
        stage_f(q)
    for copy in local[done:]:
        copy.wait()
    for copy in outs:
        copy.wait()
    wire.drain()


def add_into(dst, terms):
    count, rows, width = dst.shape
    part = min(width, 1024)

    def body(i, carry):
        for low in range(0, width, part):
            where = (i, slice(None), pl.ds(low, part))
            total = terms[0][where].astype(jnp.float32)
            for term in terms[1:]:
                total = total + term[where].astype(jnp.float32)
            dst[where] = total.astype(jnp.bfloat16)
        return carry

    lax.fori_loop(0, count, body, 0)


def return_kernel(
    part_ref, out_ref, from_core, from_x, from_z, landed, send_sems, recv_sems,
):
    x, z, c, dev = place()
    count = lax.axis_size("section")
    section = lax.axis_index("section")
    me = lax.axis_index("expert")
    before = {"section": lax.rem(section + count - 1, count), "expert": me}
    after = {"section": lax.rem(section + 1, count), "expert": me}
    greet(
        [dev(0, 1, 0), dev(0, 3, 0), dev(1, 0, 0), dev(3, 0, 0), dev(0, 0, 1)]
        + [before, after]
    )
    wire = Wire(send_sems, recv_sems)
    here = dev(0, 0, 1)
    chunks = part_ref.shape[0]
    for q in range(chunks):
        wire.send(part_ref.at[q, 1], from_core.at[q], ("c", q), here)

    def near(q):
        return (1, 3) if q % 2 == 0 else (3, 1)

    def stage_b(q):
        wire.arrive(from_core.at[q], ("c", q), here)
        by_way, plain = near(q)
        mine = from_core.at[q]
        for dx in (2, plain, by_way, 0):
            add_into(mine.at[dx], [mine.at[dx], part_ref.at[q, 0, dx]])
            if dx == 2:
                wire.send(mine.at[2], from_x.at[q, 2], ("x", q, 2), dev(by_way, 0, 0))
            if dx == plain:
                wire.send(
                    mine.at[plain], from_x.at[q, 4 - plain], ("x", q, 4 - plain), dev(plain, 0, 0)
                )

    def stage_c(q):
        by_way, _ = near(q)
        mine = from_core.at[q]
        wire.arrive(from_x.at[q, 2], ("x", q, 2), here)
        add_into(mine.at[by_way], [mine.at[by_way], from_x.at[q, 2]])
        wire.send(
            mine.at[by_way], from_x.at[q, 4 - by_way], ("x", q, 4 - by_way), dev(by_way, 0, 0)
        )

    def stage_d(q):
        by_way, plain = near(q)
        mine = from_core.at[q, 0]
        for dx in (1, 3):
            wire.arrive(from_x.at[q, dx], ("x", q, dx), here)
        add_into(mine, [mine, from_x.at[q, 1], from_x.at[q, 3]])
        wire.send(mine.at[2], from_z.at[q, 2], ("z", q, 2), dev(0, by_way, 0))
        wire.send(mine.at[plain], from_z.at[q, 4 - plain], ("z", q, 4 - plain), dev(0, plain, 0))

    def stage_e(q):
        by_way, _ = near(q)
        mine = from_core.at[q, 0]
        wire.arrive(from_z.at[q, 2], ("z", q, 2), here)
        one = pl.ds(by_way, 1)
        add_into(mine.at[one], [mine.at[one], from_z.at[q, pl.ds(2, 1)]])
        wire.send(
            mine.at[by_way], from_z.at[q, 4 - by_way], ("z", q, 4 - by_way), dev(0, by_way, 0)
        )

    def stage_f(q):
        mine = from_core.at[q, 0, pl.ds(0, 1)]
        for dz in (1, 3):
            wire.arrive(from_z.at[q, dz], ("z", q, dz), here)
        add_into(mine, [mine, from_z.at[q, pl.ds(1, 1)], from_z.at[q, pl.ds(3, 1)]])
        wire.send(from_core.at[q, 0, 0], landed.at[q], ("s", q), before)

    stages = (stage_b, stage_c, stage_d, stage_e, stage_f)
    for step in range(chunks + len(stages) - 1):
        for lag, stage in enumerate(stages):
            if 0 <= step - lag < chunks:
                stage(step - lag)
    for q in range(chunks):
        wire.arrive(landed.at[q], ("s", q), here)
        out_ref[q] = landed[q]
    wire.drain()


def on_device(grad_out, pre_act, route_ids, route_gate, w_gate, w_up, w_down):
    members = lax.axis_size("expert")
    group = members // EXPERTS
    tokens = grad_out.shape[1]
    width = grad_out.shape[2]
    hid = w_down.shape[1]
    cap = 3 * tokens // 8
    chunks = tokens // ROWS
    bf16 = jnp.bfloat16
    f32 = jnp.float32
    route = route_ids[0]
    saved = pre_act[0].reshape(tokens * 2, -1)
    experts = jnp.arange(EXPERTS, dtype=jnp.int32)
    hits = route[:, :, None] == experts
    named = jnp.any(hits, axis=1).astype(jnp.int32)
    slot = jnp.where(named > 0, jnp.cumsum(named, axis=0) - 1, -1)
    gate_te = jnp.sum(jnp.where(hits, route_gate[0][:, :, None].astype(f32), 0.0), axis=1)
    slot_tk = jnp.where(hits, slot[:, None, :], -1).reshape(tokens * 2, EXPERTS)
    pick = slot_tk.T[:, None, :] == jnp.arange(cap, dtype=jnp.int32)[None, :, None]
    rows = jnp.dot(
        pick.astype(bf16).reshape(EXPERTS * cap, tokens * 2), saved, preferred_element_type=f32
    ).astype(bf16)
    rows = rows.reshape(EXPERTS, cap, 2, group, hid).transpose(0, 3, 1, 2, 4)
    rows = rows.reshape(4, 4, 2, cap, 2 * hid)
    meta = jnp.concatenate([slot.astype(f32), gate_te], axis=1).T
    meta = jnp.pad(meta, ((0, 0), (0, 128 - tokens)))
    up = grad_out[0].reshape(chunks, ROWS, width)

    vm = pl.BlockSpec(memory_space=VMEM)
    anywhere = pl.BlockSpec(memory_space=pl.ANY)
    dma = pltpu.SemaphoreType.DMA
    all_up, acts, all_meta = pl.pallas_call(
        dispatch_kernel,
        out_shape=(
            jax.ShapeDtypeStruct((chunks, 2, 4, 4, ROWS, width), bf16),
            jax.ShapeDtypeStruct((2, 4, 4, cap, 2 * hid), bf16),
            jax.ShapeDtypeStruct((2, 4, 4, 2 * EXPERTS, 128), f32),
        ),
        in_specs=[vm] * 3,
        out_specs=(anywhere,) * 3,
        scratch_shapes=[
            VMEM((chunks, 2, 4, 4, ROWS, width), bf16),
            VMEM((2, 4, 4, 2 * EXPERTS, 128), f32),
            VMEM((2, 4, 4, cap, 2 * hid), bf16),
            VMEM((2, 4, 4, cap, 2 * hid), bf16),
            VMEM((2, 4, cap, 2 * hid), bf16),
            dma((12 + 16 * (chunks + 1),)),
            dma((12 + 16 * (chunks + 1),)),
            dma((3 + 2 * (chunks + 1),)),
        ],
        compiler_params=pltpu.CompilerParams(
            collective_id=0, has_side_effects=True, vmem_limit_bytes=56 << 20
        ),
        name="dispatch",
    )(up, rows, meta)

    all_up = all_up.reshape(members * tokens, width)
    acts = acts.reshape(members, cap, 2 * hid)
    all_meta = all_meta.reshape(members, 2, EXPERTS, 128)[..., :tokens]
    mine = lax.dynamic_index_in_dim(
        all_meta, lax.axis_index("expert") // group, axis=2, keepdims=False
    )
    rank = mine[:, 0].reshape(members, chunks, ROWS).transpose(1, 0, 2)
    gate = mine[:, 1].reshape(members, chunks, ROWS).transpose(1, 0, 2).reshape(-1, 1)
    expand = (rank[..., None] == jnp.arange(cap, dtype=f32)).astype(bf16)
    spread = jnp.einsum("qstc,scx->qstx", expand, acts, preferred_element_type=f32)
    spread = spread.reshape(members * tokens, 2 * hid)
    a = spread[:, :hid]
    b = spread[:, hid:]
    last = (((1,), (1,)), ((), ()))
    grad_h = gate * lax.dot_general(all_up, w_down[0], last, preferred_element_type=f32)
    sig = jax.nn.sigmoid(a)
    silu = a * sig
    grad_a = (grad_h * b * sig * (1.0 + a * (1.0 - sig))).astype(bf16)
    grad_b = (grad_h * silu).astype(bf16)
    scaled = (gate * silu * b).astype(bf16)
    back = lax.dot_general(grad_a, w_gate[0], last, preferred_element_type=f32)
    back = back + lax.dot_general(grad_b, w_up[0], last, preferred_element_type=f32)
    back = back.astype(bf16).reshape(chunks, 2, 4, 4, ROWS, width)
    grad_down = lax.dot_general(
        scaled, all_up, (((0,), (0,)), ((), ())), preferred_element_type=f32
    ).astype(bf16)

    block = (ROWS, width)
    grad_in = pl.pallas_call(
        return_kernel,
        out_shape=jax.ShapeDtypeStruct((chunks,) + block, bf16),
        in_specs=[vm],
        out_specs=vm,
        scratch_shapes=[
            VMEM((chunks, 4, 4) + block, bf16),
            VMEM((chunks, 4, 4) + block, bf16),
            VMEM((chunks, 4) + block, bf16),
            VMEM((chunks,) + block, bf16),
            dma((8 * chunks,)),
            dma((8 * chunks,)),
        ],
        compiler_params=pltpu.CompilerParams(
            collective_id=1, has_side_effects=True, vmem_limit_bytes=56 << 20
        ),
        name="give_back",
    )(back)
    return grad_in.reshape(1, tokens, width), grad_down[None]


def solution(mesh):
    tok = P("section", "expert", None)
    return jax.shard_map(
        on_device,
        mesh=mesh,
        in_specs=(
            tok,
            P("section", "expert", None, None, None),
            tok,
            tok,
            P("section", None, "expert"),
            P("section", None, "expert"),
            tok,
        ),
        out_specs=(tok, tok),
        check_vma=False,
    )
```

```python
import functools

import jax
import jax.numpy as jnp
from jax import lax
from jax.experimental import pallas as pl
from jax.experimental.pallas import tpu as pltpu
from jax.sharding import PartitionSpec as P

EXPERTS = 8
ROWS = 16
MESH = pl.DeviceIdType.MESH
VMEM = pltpu.VMEM


class Wire:
    def __init__(self, send_sems, recv_sems):
        self.send_sems = send_sems
        self.recv_sems = recv_sems
        self.sent = []
        self.used = {}

    def recv_sem(self, key):
        if key not in self.used:
            self.used[key] = len(self.used)
        return self.recv_sems.at[self.used[key]]

    def send(self, src, dst, key, device):
        copy = pltpu.make_async_remote_copy(
            src_ref=src,
            dst_ref=dst,
            send_sem=self.send_sems.at[len(self.sent)],
            recv_sem=self.recv_sem(key),
            device_id=device,
            device_id_type=MESH,
        )
        copy.start()
        self.sent.append(copy)

    def arrive(self, dst, key, device):
        pltpu.make_async_remote_copy(
            src_ref=dst,
            dst_ref=dst,
            send_sem=self.send_sems.at[0],
            recv_sem=self.recv_sem(key),
            device_id=device,
            device_id_type=MESH,
        ).wait_recv()

    def drain(self):
        for copy in self.sent:
            copy.wait_send()


def place():
    me = lax.axis_index("expert")
    x = me // 8
    z = lax.rem(me // 2, 4)
    c = lax.rem(me, 2)

    def dev(dx, dz, dc):
        core = c if dc == 0 else 1 - c
        return {"expert": lax.rem(x + dx, 4) * 8 + lax.rem(z + dz, 4) * 2 + core}

    return x, z, c, dev


def greet(devices):
    barrier = pltpu.get_barrier_semaphore()
    for device in devices:
        pl.semaphore_signal(barrier, inc=1, device_id=device, device_id_type=MESH)
    pl.semaphore_wait(barrier, len(devices))


def add_into(dst, terms):
    count, rows, width = dst.shape
    part = min(width, 1024)

    def body(i, carry):
        for low in range(0, width, part):
            where = (i, slice(None), pl.ds(low, part))
            total = terms[0][where].astype(jnp.float32)
            for term in terms[1:]:
                total = total + term[where].astype(jnp.float32)
            dst[where] = total.astype(jnp.bfloat16)
        return carry

    lax.fori_loop(0, count, body, 0)


def layer_kernel(
    up_ref, slots_ref, meta_ref, w_gate_ref, w_up_ref, w_down_ref, out_ref, down_ref,
    up, meta, held, acts, far, w_gate, w_up, w_down, coef_a, coef_b, scaled, grad_a, grad_b,
    part, from_core, from_x, from_z, landed, send_sems, recv_sems, copy_sems,
):
    x, z, c, dev = place()
    count = lax.axis_size("section")
    section = lax.axis_index("section")
    me = lax.axis_index("expert")
    before = {"section": lax.rem(section + count - 1, count), "expert": me}
    after = {"section": lax.rem(section + 1, count), "expert": me}
    here = dev(0, 0, 1)
    chunks, rows, width = up_ref.shape
    hid = w_down_ref.shape[0]
    cap = acts.shape[3]
    bf16 = jnp.bfloat16
    f32 = jnp.float32
    wire = Wire(send_sems, recv_sems)
    local = {}

    def keep(key, src, dst):
        copy = pltpu.make_async_copy(src, dst, copy_sems.at[len(local)])
        copy.start()
        local[key] = copy

    keep("w_down", w_down_ref, w_down)
    keep("w_gate", w_gate_ref, w_gate)
    keep("w_up", w_up_ref, w_up)
    greet(
        [dev(0, 1, 0), dev(0, 3, 0), dev(0, 1, 1), dev(0, 3, 1)]
        + [dev(1, 0, 0), dev(2, 0, 0), dev(3, 0, 0), here, before, after]
    )

    ahead = 1 + 2 * c
    behind = 3 - 2 * c
    core = (c, 1 - c)

    def slots_start():
        far_z = lax.rem(z + 2, 4)
        for dc in (0, 1):
            step = ahead if dc == 0 else behind
            wire.send(slots_ref.at[:, far_z, core[dc]], far.at[dc], ("far", dc), dev(0, step, dc))
        for step in (1, 3):
            for dc in (0, 1):
                wire.send(
                    slots_ref.at[:, lax.rem(z + step, 4), core[dc]],
                    held.at[dc, 4 - step],
                    ("held", dc, 4 - step),
                    dev(0, step, dc),
                )
        wire.send(slots_ref.at[:, z, core[1]], held.at[1, 0], ("held", 1, 0), here)
        keep("slots", slots_ref.at[:, z, c], held.at[0, 0])

    def slots_far():
        for dc in (0, 1):
            wire.arrive(far.at[dc], ("far", dc), here)
            wire.send(far.at[dc], held.at[dc, 2], ("held", dc, 2), dev(0, ahead, 0))

    def slots_x():
        local["slots"].wait()
        for dc in (0, 1):
            for dz in range(4):
                if (dc, dz) != (0, 0):
                    wire.arrive(held.at[dc, dz], ("held", dc, dz), here)
        for dx in (1, 3, 2):
            wire.send(
                held.at[:, :, lax.rem(x + dx, 4)],
                acts.at[:, (4 - dx) % 4],
                ("acts", (4 - dx) % 4),
                dev(dx, 0, 0),
            )
        keep("acts", held.at[:, :, x], acts.at[:, 0])

    def view(q):
        if q < 0:
            return meta_ref, lambda dc, dx, *dz: meta.at[(dc, dx) + dz]
        return up_ref.at[q], lambda dc, dx, *dz: up.at[(q, dc, dx) + dz]

    def pair(q):
        return (1, 3) if q % 2 == 0 else (3, 1)

    def stage_a(q):
        mine, at = view(q)
        wire.send(mine, at(0, 0, 3), ("z", q, 3), dev(0, 1, 0))
        wire.send(mine, at(0, 0, 1), ("z", q, 1), dev(0, 3, 0))
        wire.send(mine, at(0, 3, 0), ("x", q, 3, 0), dev(1, 0, 0))
        wire.send(mine, at(0, 1, 0), ("x", q, 1, 0), dev(3, 0, 0))
        keep(q, mine, at(0, 0, 0))

    def along_x(q, dz):
        _, at = view(q)
        wire.send(at(0, 0, dz), at(0, 3, dz), ("x", q, 3, dz), dev(1, 0, 0))
        wire.send(at(0, 0, dz), at(0, 1, dz), ("x", q, 1, dz), dev(3, 0, 0))

    def stage_b(q):
        _, at = view(q)
        by_way, plain = pair(q)
        for near in (by_way, plain):
            wire.arrive(at(0, 0, near), ("z", q, near), here)
            if near == by_way:
                wire.send(at(0, 0, near), at(0, 0, 2), ("z", q, 2), dev(0, 4 - near, 0))
            along_x(q, near)

    def stage_c(q):
        _, at = view(q)
        wire.arrive(at(0, 0, 2), ("z", q, 2), here)
        along_x(q, 2)
        local[q].wait()
        wire.send(at(0, 0), at(1, 0), ("c", q, 0), here)

    def stage_d(q):
        _, at = view(q)
        by_way, plain = pair(q)
        for near in (by_way, plain):
            for dz in range(4):
                wire.arrive(at(0, near, dz), ("x", q, near, dz), here)
            if near == by_way:
                wire.send(at(0, near), at(0, 2), ("x", q, 2), dev(4 - near, 0, 0))
            wire.send(at(0, near), at(1, near), ("c", q, near), here)

    def stage_e(q):
        _, at = view(q)
        wire.arrive(at(0, 2), ("x", q, 2), here)
        wire.send(at(0, 2), at(1, 2), ("c", q, 2), here)

    def stage_f(q):
        _, at = view(q)
        for dx in range(4):
            wire.arrive(at(1, dx), ("c", q, dx), here)

    def spread():
        local["acts"].wait()
        for dx in (1, 3, 2):
            wire.arrive(acts.at[:, dx], ("acts", dx), here)
        expert = me // 4
        tokens = chunks * rows
        first = (((0,), (0,)), ((), ()))

        def body(i, carry):
            dc = i // 4
            dx = lax.rem(i, 4)
            for dz in range(4):
                slot = lax.broadcasted_iota(jnp.int32, (cap, 128), 0).astype(f32)
                hit = slot == meta[dc, dx, dz, pl.ds(expert, 1), :]
                gate = meta[dc, dx, dz, pl.ds(expert + EXPERTS, 1), :]
                pick = jnp.where(hit, 1.0, 0.0).astype(bf16)
                gate_pick = jnp.where(hit, gate, 0.0).astype(bf16)
                both = lax.dot_general(pick, acts[dc, dx, dz], first, preferred_element_type=f32)
                g = lax.dot_general(
                    gate_pick, jnp.ones((cap, hid), bf16), first, preferred_element_type=f32
                )[:tokens]
                a = both[:tokens, :hid]
                b = both[:tokens, hid:]
                sig = jax.nn.sigmoid(a)
                silu = g * (a * sig)
                slope = g * b * sig * (1.0 + a * (1.0 - sig))
                third = (silu * b).astype(bf16)
                at = pl.ds(pl.multiple_of(dx * (4 * rows) + dz * rows, rows), rows)
                for q in range(chunks):
                    mine = slice(q * rows, (q + 1) * rows)
                    coef_a[q, dc, at, :] = slope[mine]
                    coef_b[q, dc, at, :] = silu[mine]
                    scaled[q, dc, at, :] = third[mine]
            return carry

        lax.fori_loop(0, 8, body, 0)

    last = (((1,), (1,)), ((), ()))
    step = 256

    def stage_g(q):
        for dc in (1, 0):
            mine = up[q, dc].reshape(16 * rows, width)
            grad_h = lax.dot_general(mine, w_down[...], last, preferred_element_type=f32)
            grad_a[...] = (grad_h * coef_a[q, dc]).astype(bf16)
            grad_b[...] = (grad_h * coef_b[q, dc]).astype(bf16)

            def body(n, carry):
                cols = pl.ds(pl.multiple_of(n * step, step), step)
                total = lax.dot_general(
                    grad_a[...], w_gate[cols, :], last, preferred_element_type=f32
                ) + lax.dot_general(grad_b[...], w_up[cols, :], last, preferred_element_type=f32)
                part[q, dc, :, :, :, cols] = total.astype(bf16).reshape(4, 4, rows, step)
                return carry

            lax.fori_loop(0, width // step, body, 0)
            if dc == 1:
                wire.send(part.at[q, 1], from_core.at[q], ("back c", q), here)

    def weight_grad():
        left = scaled[...].reshape(32 * chunks * rows, hid)
        wide = 512

        def body(n, carry):
            cols = pl.ds(pl.multiple_of(n * wide, wide), wide)
            down_ref[:, cols] = lax.dot_general(
                left,
                up[:, :, :, :, :, cols].reshape(32 * chunks * rows, wide),
                (((0,), (0,)), ((), ())),
                preferred_element_type=f32,
            ).astype(bf16)
            return carry

        lax.fori_loop(0, width // wide, body, 0)

    def back_b(q):
        wire.arrive(from_core.at[q], ("back c", q), here)
        by_way, plain = pair(q)
        mine = from_core.at[q]
        for dx in (2, plain, by_way, 0):
            add_into(mine.at[dx], [mine.at[dx], part.at[q, 0, dx]])
            if dx == 2:
                wire.send(mine.at[2], from_x.at[q, 2], ("back x", q, 2), dev(by_way, 0, 0))
            if dx == plain:
                wire.send(
                    mine.at[plain],
                    from_x.at[q, 4 - plain],
                    ("back x", q, 4 - plain),
                    dev(plain, 0, 0),
                )

    def back_c(q):
        by_way, _ = pair(q)
        mine = from_core.at[q]
        wire.arrive(from_x.at[q, 2], ("back x", q, 2), here)
        add_into(mine.at[by_way], [mine.at[by_way], from_x.at[q, 2]])
        wire.send(
            mine.at[by_way], from_x.at[q, 4 - by_way], ("back x", q, 4 - by_way), dev(by_way, 0, 0)
        )

    def back_d(q):
        by_way, plain = pair(q)
        mine = from_core.at[q, 0]
        for dx in (1, 3):
            wire.arrive(from_x.at[q, dx], ("back x", q, dx), here)
        add_into(mine, [mine, from_x.at[q, 1], from_x.at[q, 3]])
        wire.send(mine.at[2], from_z.at[q, 2], ("back z", q, 2), dev(0, by_way, 0))
        wire.send(
            mine.at[plain], from_z.at[q, 4 - plain], ("back z", q, 4 - plain), dev(0, plain, 0)
        )

    def back_e(q):
        by_way, _ = pair(q)
        mine = from_core.at[q, 0]
        wire.arrive(from_z.at[q, 2], ("back z", q, 2), here)
        one = pl.ds(by_way, 1)
        add_into(mine.at[one], [mine.at[one], from_z.at[q, pl.ds(2, 1)]])
        wire.send(
            mine.at[by_way], from_z.at[q, 4 - by_way], ("back z", q, 4 - by_way), dev(0, by_way, 0)
        )

    def back_f(q):
        mine = from_core.at[q, 0, pl.ds(0, 1)]
        for dz in (1, 3):
            wire.arrive(from_z.at[q, dz], ("back z", q, dz), here)
        add_into(mine, [mine, from_z.at[q, pl.ds(1, 1)], from_z.at[q, pl.ds(3, 1)]])
        wire.send(from_core.at[q, 0, 0], landed.at[q], ("s", q), before)

    slots_start()
    stage_a(-1)
    stage_a(0)
    stage_a(1)
    slots_far()
    stage_b(-1)
    slots_x()
    stage_c(-1)
    stage_b(0)
    stage_a(2)
    stage_d(-1)
    stage_e(-1)
    stage_f(-1)
    spread()
    stage_b(1)
    stage_a(3)
    for key in ("w_down", "w_gate", "w_up"):
        local[key].wait()
    plan = "C0 D0 B2 C1 E0 F0 G0 D1 B3 b0 E1 F1 G1 c0 C2 D2 b1 C3 E2 F2 G2 d0 c1 D3 b2 E3 F3 G3"
    plan += " d1 e0 c2 b3 d2 e1 f0 c3 W d3 e2 f1 e3 f2 f3"
    table = {
        "B": stage_b, "C": stage_c, "D": stage_d, "E": stage_e, "F": stage_f, "G": stage_g,
        "b": back_b, "c": back_c, "d": back_d, "e": back_e, "f": back_f,
    }
    for entry in plan.split():
        if entry == "W":
            weight_grad()
        else:
            table[entry[0]](int(entry[1]))
    for q in range(chunks):
        wire.arrive(landed.at[q], ("s", q), here)
        out_ref[q] = landed[q]
    wire.drain()


def on_device(grad_out, pre_act, route_ids, route_gate, w_gate, w_up, w_down):
    members = lax.axis_size("expert")
    group = members // EXPERTS
    tokens = grad_out.shape[1]
    width = grad_out.shape[2]
    hid = w_down.shape[1]
    cap = 3 * tokens // 8
    chunks = tokens // ROWS
    bf16 = jnp.bfloat16
    f32 = jnp.float32
    route = route_ids[0]
    saved = pre_act[0].reshape(tokens * 2, -1)
    experts = jnp.arange(EXPERTS, dtype=jnp.int32)
    hits = route[:, :, None] == experts
    named = jnp.any(hits, axis=1).astype(jnp.int32)
    slot = jnp.where(named > 0, jnp.cumsum(named, axis=0) - 1, -1)
    gate_te = jnp.sum(jnp.where(hits, route_gate[0][:, :, None].astype(f32), 0.0), axis=1)
    slot_tk = jnp.where(hits, slot[:, None, :], -1).reshape(tokens * 2, EXPERTS)
    pick = slot_tk.T[:, None, :] == jnp.arange(cap, dtype=jnp.int32)[None, :, None]
    rows = jnp.dot(
        pick.astype(bf16).reshape(EXPERTS * cap, tokens * 2), saved, preferred_element_type=f32
    ).astype(bf16)
    rows = rows.reshape(EXPERTS, cap, 2, group, hid).transpose(0, 3, 1, 2, 4)
    rows = rows.reshape(4, 4, 2, cap, 2 * hid)
    meta = jnp.concatenate([slot.astype(f32), gate_te], axis=1).T
    meta = jnp.pad(meta, ((0, 0), (0, 128 - tokens)), constant_values=-1.0)
    up = grad_out[0].reshape(chunks, ROWS, width)

    vm = pl.BlockSpec(memory_space=VMEM)
    anywhere = pl.BlockSpec(memory_space=pl.ANY)
    dma = pltpu.SemaphoreType.DMA
    block = (ROWS, width)
    copies = 12 + 16 * (chunks + 1) + 8 * chunks
    grad_in, grad_down = pl.pallas_call(
        layer_kernel,
        out_shape=(
            jax.ShapeDtypeStruct((chunks,) + block, bf16),
            jax.ShapeDtypeStruct((hid, width), bf16),
        ),
        in_specs=[vm] * 3 + [anywhere] * 3,
        out_specs=(vm, vm),
        scratch_shapes=[
            VMEM((chunks, 2, 4, 4) + block, bf16),
            VMEM((2, 4, 4, 2 * EXPERTS, 128), f32),
            VMEM((2, 4, 4, cap, 2 * hid), bf16),
            VMEM((2, 4, 4, cap, 2 * hid), bf16),
            VMEM((2, 4, cap, 2 * hid), bf16),
            VMEM((width, hid), bf16),
            VMEM((width, hid), bf16),
            VMEM((hid, width), bf16),
            VMEM((chunks, 2, 16 * ROWS, hid), f32),
            VMEM((chunks, 2, 16 * ROWS, hid), f32),
            VMEM((chunks, 2, 16 * ROWS, hid), bf16),
            VMEM((16 * ROWS, hid), bf16),
            VMEM((16 * ROWS, hid), bf16),
            VMEM((chunks, 2, 4, 4) + block, bf16),
            VMEM((chunks, 4, 4) + block, bf16),
            VMEM((chunks, 4, 4) + block, bf16),
            VMEM((chunks, 4) + block, bf16),
            VMEM((chunks,) + block, bf16),
            dma((copies,)),
            dma((copies,)),
            dma((chunks + 6,)),
        ],
        compiler_params=pltpu.CompilerParams(
            collective_id=0, has_side_effects=True, vmem_limit_bytes=60 << 20
        ),
        name="layer",
    )(up, rows, meta, w_gate[0], w_up[0], w_down[0])
    return grad_in.reshape(1, tokens, width), grad_down[None]


def solution(mesh):
    tok = P("section", "expert", None)
    return jax.shard_map(
        on_device,
        mesh=mesh,
        in_specs=(
            tok,
            P("section", "expert", None, None, None),
            tok,
            tok,
            P("section", None, "expert"),
            P("section", None, "expert"),
            tok,
        ),
        out_specs=(tok, tok),
        check_vma=False,
    )
```

```python
import functools

import jax
import jax.numpy as jnp
from jax import lax
from jax.experimental import pallas as pl
from jax.experimental.pallas import tpu as pltpu
from jax.sharding import PartitionSpec as P

EXPERTS = 8
ROWS = 16
MESH = pl.DeviceIdType.MESH
VMEM = pltpu.VMEM


class Wire:
    def __init__(self, send_sems, recv_sems):
        self.send_sems = send_sems
        self.recv_sems = recv_sems
        self.sent = []
        self.used = {}

    def recv_sem(self, key):
        if key not in self.used:
            self.used[key] = len(self.used)
        return self.recv_sems.at[self.used[key]]

    def send(self, src, dst, key, device):
        copy = pltpu.make_async_remote_copy(
            src_ref=src,
            dst_ref=dst,
            send_sem=self.send_sems.at[len(self.sent)],
            recv_sem=self.recv_sem(key),
            device_id=device,
            device_id_type=MESH,
        )
        copy.start()
        self.sent.append(copy)

    def arrive(self, dst, key, device):
        pltpu.make_async_remote_copy(
            src_ref=dst,
            dst_ref=dst,
            send_sem=self.send_sems.at[0],
            recv_sem=self.recv_sem(key),
            device_id=device,
            device_id_type=MESH,
        ).wait_recv()

    def drain(self):
        for copy in self.sent:
            copy.wait_send()


def place():
    me = lax.axis_index("expert")
    x = me // 8
    z = lax.rem(me // 2, 4)
    c = lax.rem(me, 2)

    def dev(dx, dz, dc):
        core = c if dc == 0 else 1 - c
        return {"expert": lax.rem(x + dx, 4) * 8 + lax.rem(z + dz, 4) * 2 + core}

    return x, z, c, dev


def greet(devices):
    barrier = pltpu.get_barrier_semaphore()
    for device in devices:
        pl.semaphore_signal(barrier, inc=1, device_id=device, device_id_type=MESH)
    pl.semaphore_wait(barrier, len(devices))


def add_block(dst, terms, low, size):
    part = min(size, 1024)
    for at in range(low, low + size, part):
        cols = pl.ds(at, part)
        total = terms[0][:, cols].astype(jnp.float32)
        for term in terms[1:]:
            total = total + term[:, cols].astype(jnp.float32)
        dst[:, cols] = total.astype(jnp.bfloat16)


def layer_kernel(
    up_ref, slots_ref, meta_ref, w_gate_ref, w_up_ref, w_down_ref, out_ref, down_ref,
    up, meta, held, acts, w_gate, w_up, w_down, coef_a, coef_b, scaled, grad_a, grad_b,
    part, from_core, from_x, from_z, landed, send_sems, recv_sems, copy_sems,
):
    x, z, c, dev = place()
    count = lax.axis_size("section")
    section = lax.axis_index("section")
    me = lax.axis_index("expert")
    before = {"section": lax.rem(section + count - 1, count), "expert": me}
    after = {"section": lax.rem(section + 1, count), "expert": me}
    here = dev(0, 0, 1)
    chunks, rows, width = up_ref.shape
    hid = w_down_ref.shape[0]
    cap = acts.shape[3]
    bf16 = jnp.bfloat16
    f32 = jnp.float32
    wire = Wire(send_sems, recv_sems)
    local = {}

    def keep(key, src, dst):
        copy = pltpu.make_async_copy(src, dst, copy_sems.at[len(local)])
        copy.start()
        local[key] = copy

    keep("w_down", w_down_ref, w_down)
    keep("w_gate", w_gate_ref, w_gate)
    keep("w_up", w_up_ref, w_up)
    greet(
        [dev(0, dz, dc) for dz in (1, 2, 3) for dc in (0, 1)]
        + [dev(1, 0, 0), dev(2, 0, 0), dev(3, 0, 0), here, before, after]
    )

    core = (c, 1 - c)

    def slots_start():
        for dz in (1, 3, 2):
            for dc in (0, 1):
                wire.send(
                    slots_ref.at[:, lax.rem(z + dz, 4), core[dc]],
                    held.at[dc, 4 - dz],
                    ("held", dc, 4 - dz),
                    dev(0, dz, dc),
                )
        wire.send(slots_ref.at[:, z, core[1]], held.at[1, 0], ("held", 1, 0), here)
        keep("slots", slots_ref.at[:, z, c], held.at[0, 0])

    def slots_x(dc, dz):
        if (dc, dz) == (0, 0):
            local["slots"].wait()
        else:
            wire.arrive(held.at[dc, dz], ("held", dc, dz), here)
        for dx in (2, 1, 3):
            wire.send(
                held.at[dc, dz, lax.rem(x + dx, 4)],
                acts.at[dc, 4 - dx, dz],
                ("acts", dc, dz, dx),
                dev(dx, 0, 0),
            )

    def view(q):
        if q < 0:
            return meta_ref, lambda dc, dx, *dz: meta.at[(dc, dx) + dz]
        return up_ref.at[q], lambda dc, dx, *dz: up.at[(q, dc, dx) + dz]

    def pair(q):
        return (1, 3) if q % 2 == 0 else (3, 1)

    def stage_a(q):
        mine, at = view(q)
        wire.send(mine, at(0, 0, 3), ("z", q, 3), dev(0, 1, 0))
        wire.send(mine, at(0, 0, 1), ("z", q, 1), dev(0, 3, 0))
        wire.send(mine, at(0, 3, 0), ("x", q, 3, 0), dev(1, 0, 0))
        wire.send(mine, at(0, 1, 0), ("x", q, 1, 0), dev(3, 0, 0))
        keep(q, mine, at(0, 0, 0))

    def along_x(q, dz):
        _, at = view(q)
        wire.send(at(0, 0, dz), at(0, 3, dz), ("x", q, 3, dz), dev(1, 0, 0))
        wire.send(at(0, 0, dz), at(0, 1, dz), ("x", q, 1, dz), dev(3, 0, 0))

    def stage_b(q, near):
        _, at = view(q)
        wire.arrive(at(0, 0, near), ("z", q, near), here)
        if near == pair(q)[0]:
            wire.send(at(0, 0, near), at(0, 0, 2), ("z", q, 2), dev(0, 4 - near, 0))
        along_x(q, near)

    def stage_c(q):
        _, at = view(q)
        wire.arrive(at(0, 0, 2), ("z", q, 2), here)
        along_x(q, 2)
        local[q].wait()
        wire.send(at(0, 0), at(1, 0), ("c", q, 0), here)

    def stage_d(q, dz):
        _, at = view(q)
        near = pair(q)[0]
        wire.arrive(at(0, near, dz), ("x", q, near, dz), here)
        wire.send(at(0, near, dz), at(0, 2, dz), ("x", q, 2, dz), dev(4 - near, 0, 0))

    def stage_h(q):
        _, at = view(q)
        plain = pair(q)[1]
        for dz in range(4):
            wire.arrive(at(0, plain, dz), ("x", q, plain, dz), here)
        wire.send(at(0, plain), at(1, plain), ("c", q, plain), here)

    def stage_i(q):
        _, at = view(q)
        near = pair(q)[0]
        wire.send(at(0, near), at(1, near), ("c", q, near), here)

    def stage_e(q):
        _, at = view(q)
        for dz in range(4):
            wire.arrive(at(0, 2, dz), ("x", q, 2, dz), here)
        wire.send(at(0, 2), at(1, 2), ("c", q, 2), here)

    def stage_f(q):
        _, at = view(q)
        for dx in range(4):
            wire.arrive(at(1, dx), ("c", q, dx), here)

    expert = me // 4
    tokens = chunks * rows
    first = (((0,), (0,)), ((), ()))

    def spread(dc, dz):
        for dx in (1, 3, 2):
            wire.arrive(acts.at[dc, 4 - dx, dz], ("acts", dc, dz, dx), here)
        for dx in range(4):
            act = held[dc, dz, x] if dx == 0 else acts[dc, dx, dz]
            slot = lax.broadcasted_iota(jnp.int32, (cap, 128), 0).astype(f32)
            hit = slot == meta[dc, dx, dz, pl.ds(expert, 1), :]
            gate = meta[dc, dx, dz, pl.ds(expert + EXPERTS, 1), :]
            pick = jnp.where(hit, 1.0, 0.0).astype(bf16)
            gate_pick = jnp.where(hit, gate, 0.0).astype(bf16)
            both = lax.dot_general(pick, act, first, preferred_element_type=f32)
            g = lax.dot_general(
                gate_pick, jnp.ones((cap, hid), bf16), first, preferred_element_type=f32
            )[:tokens]
            a = both[:tokens, :hid]
            b = both[:tokens, hid:]
            sig = jax.nn.sigmoid(a)
            silu = g * (a * sig)
            slope = g * b * sig * (1.0 + a * (1.0 - sig))
            third = (silu * b).astype(bf16)
            low = (dx * 4 + dz) * rows
            for q in range(chunks):
                mine = slice(q * rows, (q + 1) * rows)
                coef_a[q, dc, low : low + rows, :] = slope[mine]
                coef_b[q, dc, low : low + rows, :] = silu[mine]
                scaled[q, dc, low : low + rows, :] = third[mine]

    last = (((1,), (1,)), ((), ()))
    step = 256

    def stage_g(q, dc):
        mine = up[q, dc].reshape(16 * rows, width)
        grad_h = lax.dot_general(mine, w_down[...], last, preferred_element_type=f32)
        grad_a[...] = (grad_h * coef_a[q, dc]).astype(bf16)
        grad_b[...] = (grad_h * coef_b[q, dc]).astype(bf16)

        def body(n, carry):
            cols = pl.ds(pl.multiple_of(n * step, step), step)
            total = lax.dot_general(
                grad_a[...], w_gate[cols, :], last, preferred_element_type=f32
            ) + lax.dot_general(grad_b[...], w_up[cols, :], last, preferred_element_type=f32)
            part[q, dc, :, :, :, cols] = total.astype(bf16).reshape(4, 4, rows, step)
            return carry

        lax.fori_loop(0, width // step, body, 0)
        if dc == 1:
            wire.send(part.at[q, 1], from_core.at[q], ("back c", q), here)

    def weight_grad():
        left = scaled[...].reshape(32 * chunks * rows, hid)
        wide = 512

        def body(n, carry):
            cols = pl.ds(pl.multiple_of(n * wide, wide), wide)
            down_ref[:, cols] = lax.dot_general(
                left,
                up[:, :, :, :, :, cols].reshape(32 * chunks * rows, wide),
                (((0,), (0,)), ((), ())),
                preferred_element_type=f32,
            ).astype(bf16)
            return carry

        lax.fori_loop(0, width // wide, body, 0)

    def back_b(q, dz):
        by_way, plain = pair(q)
        if dz == 2:
            wire.arrive(from_core.at[q], ("back c", q), here)

        def body(dx, carry):
            mine = from_core.at[q, dx, dz]
            add_block(mine, [mine, part.at[q, 0, dx, dz]], 0, width)
            return carry

        lax.fori_loop(0, 4, body, 0)
        for dx, key, way in ((2, 2, by_way), (plain, 4 - plain, plain)):
            wire.send(
                from_core.at[q, dx, dz], from_x.at[q, key, dz], ("back x", q, key, dz), dev(way, 0, 0)
            )

    def back_c(q, dz):
        by_way, _ = pair(q)
        mine = from_core.at[q, by_way, dz]
        wire.arrive(from_x.at[q, 2, dz], ("back x", q, 2, dz), here)
        add_block(mine, [mine, from_x.at[q, 2, dz]], 0, width)
        key = 4 - by_way
        wire.send(mine, from_x.at[q, key, dz], ("back x", q, key, dz), dev(by_way, 0, 0))

    half = width // 2

    def half_of(ref, h):
        return ref.at[:, pl.ds(h * half, half)]

    def give_z(q, dz, key, way, h):
        wire.send(
            half_of(from_core.at[q, 0, dz], h),
            half_of(from_z.at[q, key], h),
            ("back z", q, key, h),
            dev(0, way, 0),
        )

    def back_d(q, dz):
        by_way, plain = pair(q)
        mine = from_core.at[q, 0, dz]
        for dx in (1, 3):
            wire.arrive(from_x.at[q, dx, dz], ("back x", q, dx, dz), here)
        add_block(mine, [mine, from_x.at[q, 1, dz], from_x.at[q, 3, dz]], 0, width)
        for h in (0, 1):
            if dz == 2:
                give_z(q, 2, 2, by_way, h)
            if dz == plain:
                give_z(q, plain, 4 - plain, plain, h)

    def back_e(q, h):
        by_way, _ = pair(q)
        mine = from_core.at[q, 0, by_way]
        wire.arrive(half_of(from_z.at[q, 2], h), ("back z", q, 2, h), here)
        add_block(mine, [mine, from_z.at[q, 2]], h * half, half)
        give_z(q, by_way, 4 - by_way, by_way, h)

    def back_f(q, h):
        mine = from_core.at[q, 0, 0]
        for dz in (1, 3):
            wire.arrive(half_of(from_z.at[q, dz], h), ("back z", q, dz, h), here)
        add_block(mine, [mine, from_z.at[q, 1], from_z.at[q, 3]], h * half, half)
        wire.send(half_of(mine, h), half_of(landed.at[q], h), ("s", q, h), before)

    def meta_near():
        stage_b(-1, 1)
        stage_b(-1, 3)

    def meta_rest():
        stage_c(-1)
        for dz in range(4):
            stage_d(-1, dz)
        stage_h(-1)
        stage_i(-1)
        stage_e(-1)
        stage_f(-1)
        for key in ("w_down", "w_gate", "w_up"):
            local[key].wait()

    stage_a(-1)
    plan = (
        "A0 A1 M0 S",
        "X00 X10 D00 D10",
        "B03 B01 A2 D03",
        "D01 B11 B13 A3",
        "D20 D11 D13 D30",
        "X03 X01 M1 P00",
        "P10 P03 P01 X13",
        "X11 P13 P11 X12",
        "X02 P12 P02 B23",
        "C0 D23 D02 I0",
        "H0 C1 B21 E0",
        "D12 I1 H1 F0",
        "G0 D21 B33 B31",
        "g0 E1 b02 b03",
        "F1 D33 G1 C2",
        "D31 c02 g1 c03",
        "b01 b00 b12 b11",
        "D22 I2 H2 C3",
        "b13 b10 d02 d03",
        "c12 c01 c11 c00",
        "E2 H3 F2 G2",
        "g2 c13 c10 D32",
        "I3 d12 b22 b23",
        "d11 b21 b20 d01",
        "e01 d13 e00 d00",
        "d10 E3 c22 F3",
        "G3 c23 e10 g3",
        "c21 e11 c20 b32",
        "d22 b31 b33 d23",
        "b30 W c32 f10",
        "d20 f01 f00 c31",
        "d21 f11 c33 c30",
        "e20 d32 d31 e21",
        "d33 d30 f20 e30",
        "e31 f30 f21 f31",
    )
    table = {
        "A": stage_a, "B": stage_b, "C": stage_c, "D": stage_d, "E": stage_e, "F": stage_f,
        "H": stage_h, "I": stage_i, "X": slots_x, "P": spread, "S": slots_start,
        "G": lambda q: stage_g(q, 1), "g": lambda q: stage_g(q, 0), "W": weight_grad,
        "b": back_b, "c": back_c, "d": back_d, "e": back_e, "f": back_f,
        "M": lambda late: meta_rest() if late else meta_near(),
    }
    for line in plan:
        for entry in line.split():
            table[entry[0]](*[int(digit) for digit in entry[1:]])
    for q in range(chunks):
        for h in (0, 1):
            wire.arrive(half_of(landed.at[q], h), ("s", q, h), here)
        out_ref[q] = landed[q]
    wire.drain()


def on_device(grad_out, pre_act, route_ids, route_gate, w_gate, w_up, w_down):
    members = lax.axis_size("expert")
    group = members // EXPERTS
    tokens = grad_out.shape[1]
    width = grad_out.shape[2]
    hid = w_down.shape[1]
    cap = 3 * tokens // 8
    chunks = tokens // ROWS
    bf16 = jnp.bfloat16
    f32 = jnp.float32
    route = route_ids[0]
    saved = pre_act[0].reshape(tokens * 2, -1)
    experts = jnp.arange(EXPERTS, dtype=jnp.int32)
    hits = route[:, :, None] == experts
    named = jnp.any(hits, axis=1).astype(jnp.int32)
    slot = jnp.where(named > 0, jnp.cumsum(named, axis=0) - 1, -1)
    gate_te = jnp.sum(jnp.where(hits, route_gate[0][:, :, None].astype(f32), 0.0), axis=1)
    slot_tk = jnp.where(hits, slot[:, None, :], -1).reshape(tokens * 2, EXPERTS)
    pick = slot_tk.T[:, None, :] == jnp.arange(cap, dtype=jnp.int32)[None, :, None]
    rows = jnp.dot(
        pick.astype(bf16).reshape(EXPERTS * cap, tokens * 2), saved, preferred_element_type=f32
    ).astype(bf16)
    rows = rows.reshape(EXPERTS, cap, 2, group, hid).transpose(0, 3, 1, 2, 4)
    rows = rows.reshape(4, 4, 2, cap, 2 * hid)
    meta = jnp.concatenate([slot.astype(f32), gate_te], axis=1).T
    meta = jnp.pad(meta, ((0, 0), (0, 128 - tokens)), constant_values=-1.0)
    up = grad_out[0].reshape(chunks, ROWS, width)

    vm = pl.BlockSpec(memory_space=VMEM)
    anywhere = pl.BlockSpec(memory_space=pl.ANY)
    dma = pltpu.SemaphoreType.DMA
    block = (ROWS, width)
    copies = 31 + 19 * (chunks + 1) + 21 * chunks
    grad_in, grad_down = pl.pallas_call(
        layer_kernel,
        out_shape=(
            jax.ShapeDtypeStruct((chunks,) + block, bf16),
            jax.ShapeDtypeStruct((hid, width), bf16),
        ),
        in_specs=[vm] * 3 + [anywhere] * 3,
        out_specs=(vm, vm),
        scratch_shapes=[
            VMEM((chunks, 2, 4, 4) + block, bf16),
            VMEM((2, 4, 4, 2 * EXPERTS, 128), f32),
            VMEM((2, 4, 4, cap, 2 * hid), bf16),
            VMEM((2, 4, 4, cap, 2 * hid), bf16),
            VMEM((width, hid), bf16),
            VMEM((width, hid), bf16),
            VMEM((hid, width), bf16),
            VMEM((chunks, 2, 16 * ROWS, hid), f32),
            VMEM((chunks, 2, 16 * ROWS, hid), f32),
            VMEM((chunks, 2, 16 * ROWS, hid), bf16),
            VMEM((16 * ROWS, hid), bf16),
            VMEM((16 * ROWS, hid), bf16),
            VMEM((chunks, 2, 4, 4) + block, bf16),
            VMEM((chunks, 4, 4) + block, bf16),
            VMEM((chunks, 4, 4) + block, bf16),
            VMEM((chunks, 4) + block, bf16),
            VMEM((chunks,) + block, bf16),
            dma((copies,)),
            dma((copies,)),
            dma((chunks + 6,)),
        ],
        compiler_params=pltpu.CompilerParams(
            collective_id=0, has_side_effects=True, vmem_limit_bytes=60 << 20
        ),
        name="layer",
    )(up, rows, meta, w_gate[0], w_up[0], w_down[0])
    return grad_in.reshape(1, tokens, width), grad_down[None]


def solution(mesh):
    tok = P("section", "expert", None)
    return jax.shard_map(
        on_device,
        mesh=mesh,
        in_specs=(
            tok,
            P("section", "expert", None, None, None),
            tok,
            tok,
            P("section", None, "expert"),
            P("section", None, "expert"),
            tok,
        ),
        out_specs=(tok, tok),
        check_vma=False,
    )
```

```python
import functools

import jax
import jax.numpy as jnp
from jax import lax
from jax.experimental import pallas as pl
from jax.experimental.pallas import tpu as pltpu
from jax.sharding import PartitionSpec as P

EXPERTS = 8
ROWS = 16
MESH = pl.DeviceIdType.MESH
VMEM = pltpu.VMEM


class Wire:
    def __init__(self, send_sems, recv_sems):
        self.send_sems = send_sems
        self.recv_sems = recv_sems
        self.sent = []
        self.used = {}

    def recv_sem(self, key):
        if key not in self.used:
            self.used[key] = len(self.used)
        return self.recv_sems.at[self.used[key]]

    def send(self, src, dst, key, device):
        copy = pltpu.make_async_remote_copy(
            src_ref=src,
            dst_ref=dst,
            send_sem=self.send_sems.at[len(self.sent)],
            recv_sem=self.recv_sem(key),
            device_id=device,
            device_id_type=MESH,
        )
        copy.start()
        self.sent.append(copy)

    def arrive(self, dst, key, device):
        pltpu.make_async_remote_copy(
            src_ref=dst,
            dst_ref=dst,
            send_sem=self.send_sems.at[0],
            recv_sem=self.recv_sem(key),
            device_id=device,
            device_id_type=MESH,
        ).wait_recv()

    def drain(self):
        for copy in self.sent:
            copy.wait_send()


def place():
    me = lax.axis_index("expert")
    x = me // 8
    z = lax.rem(me // 2, 4)
    c = lax.rem(me, 2)

    def dev(dx, dz, dc):
        core = c if dc == 0 else 1 - c
        return {"expert": lax.rem(x + dx, 4) * 8 + lax.rem(z + dz, 4) * 2 + core}

    return x, z, c, dev


def greet(devices):
    barrier = pltpu.get_barrier_semaphore()
    for device in devices:
        pl.semaphore_signal(barrier, inc=1, device_id=device, device_id_type=MESH)
    pl.semaphore_wait(barrier, len(devices))


def add_block(dst, terms, low, size):
    part = min(size, 1024)
    for at in range(low, low + size, part):
        cols = pl.ds(at, part)
        total = terms[0][:, cols].astype(jnp.float32)
        for term in terms[1:]:
            total = total + term[:, cols].astype(jnp.float32)
        dst[:, cols] = total.astype(jnp.bfloat16)


def layer_kernel(
    up_ref, saved_ref, route_ref, gate_ref, w_gate_ref, w_up_ref, w_down_ref, out_ref, down_ref,
    up, meta, own_meta, slots, held, acts, w_gate, w_up, w_down, coef_a, coef_b, scaled, grad_a, grad_b,
    part, from_core, from_x, from_z, landed, send_sems, recv_sems, copy_sems,
):
    x, z, c, dev = place()
    count = lax.axis_size("section")
    section = lax.axis_index("section")
    me = lax.axis_index("expert")
    before = {"section": lax.rem(section + count - 1, count), "expert": me}
    after = {"section": lax.rem(section + 1, count), "expert": me}
    here = dev(0, 0, 1)
    chunks, rows, width = up_ref.shape
    hid = w_down_ref.shape[0]
    cap = acts.shape[3]
    tokens = chunks * rows
    bf16 = jnp.bfloat16
    f32 = jnp.float32
    wire = Wire(send_sems, recv_sems)
    local = {}

    def keep(key, src, dst):
        copy = pltpu.make_async_copy(src, dst, copy_sems.at[len(local)])
        copy.start()
        local[key] = copy

    keep("w_down", w_down_ref, w_down)
    keep("w_gate", w_gate_ref, w_gate)
    keep("w_up", w_up_ref, w_up)
    greet(
        [dev(0, dz, dc) for dz in (1, 2, 3) for dc in (0, 1)]
        + [dev(1, 0, 0), dev(2, 0, 0), dev(3, 0, 0), here, before, after]
    )

    core = (c, 1 - c)

    lane = lax.broadcasted_iota(jnp.int32, (EXPERTS, 2 * tokens), 1)
    hit = lane * 0 + jnp.concatenate([route_ref[0:1, :], route_ref[1:2, :]], axis=1)
    hit = hit == lax.broadcasted_iota(jnp.int32, (EXPERTS, 2 * tokens), 0)

    def routes():
        earlier = lax.broadcasted_iota(jnp.int32, (2 * tokens, 2 * tokens), 0) % tokens
        later = lax.broadcasted_iota(jnp.int32, (2 * tokens, 2 * tokens), 1) % tokens
        upto = jnp.where(earlier <= later, 1.0, 0.0).astype(bf16)
        ones = jnp.where(hit, 1.0, 0.0).astype(bf16)
        rank = jnp.dot(ones, upto, preferred_element_type=f32) - 1.0
        return jnp.where(hit, rank, -1.0)

    rank = routes()

    def meta_own():
        gates = gate_ref[...].astype(f32)
        gates = jnp.concatenate([gates[0:1, :], gates[1:2, :]], axis=1)
        gates = jnp.where(hit, jnp.broadcast_to(gates, hit.shape), 0.0)
        either = jnp.maximum(rank, pltpu.roll(rank, tokens, 1))
        own_meta[0:EXPERTS, :] = jnp.where(lane < tokens, either, -1.0)
        own_meta[EXPERTS:, :] = gates + pltpu.roll(gates, tokens, 1)

    def slots_fill():
        slot = lax.broadcasted_iota(jnp.int32, (cap, 2 * tokens), 0).astype(f32)
        picks = [
            jnp.where(slot == rank[e : e + 1, :], 1.0, 0.0) for e in range(EXPERTS)
        ]
        pick = jnp.concatenate(picks, axis=0).astype(bf16)
        side = 4 * hid
        for low in (0, side):
            taken = jnp.dot(pick, saved_ref[:, low : low + side], preferred_element_type=f32)
            for e in range(EXPERTS):
                for m in range(4):
                    piece = taken[e * cap : (e + 1) * cap, m * hid : (m + 1) * hid]
                    at = 0 if low == 0 else hid
                    slots[e // 2, 2 * (e % 2) + m // 2, m % 2, :, at : at + hid] = piece.astype(bf16)

    def slots_start():
        slots_fill()
        for dz in (1, 3, 2):
            for dc in (0, 1):
                wire.send(
                    slots.at[:, lax.rem(z + dz, 4), core[dc]],
                    held.at[dc, 4 - dz],
                    ("held", dc, 4 - dz),
                    dev(0, dz, dc),
                )
        wire.send(slots.at[:, z, core[1]], held.at[1, 0], ("held", 1, 0), here)
        keep("slots", slots.at[:, z, c], held.at[0, 0])

    def slots_x(dc, dz):
        if (dc, dz) == (0, 0):
            local["slots"].wait()
        else:
            wire.arrive(held.at[dc, dz], ("held", dc, dz), here)
        for dx in (2, 1, 3):
            wire.send(
                held.at[dc, dz, lax.rem(x + dx, 4)],
                acts.at[dc, 4 - dx, dz],
                ("acts", dc, dz, dx),
                dev(dx, 0, 0),
            )

    def view(q):
        if q < 0:
            return own_meta, lambda dc, dx, *dz: meta.at[(dc, dx) + dz]
        return up_ref.at[q], lambda dc, dx, *dz: up.at[(q, dc, dx) + dz]

    def pair(q):
        return (1, 3) if q % 2 == 0 else (3, 1)

    def stage_a(q):
        mine, at = view(q)
        wire.send(mine, at(0, 0, 3), ("z", q, 3), dev(0, 1, 0))
        wire.send(mine, at(0, 0, 1), ("z", q, 1), dev(0, 3, 0))
        wire.send(mine, at(0, 3, 0), ("x", q, 3, 0), dev(1, 0, 0))
        wire.send(mine, at(0, 1, 0), ("x", q, 1, 0), dev(3, 0, 0))
        keep(q, mine, at(0, 0, 0))

    def along_x(q, dz):
        _, at = view(q)
        wire.send(at(0, 0, dz), at(0, 3, dz), ("x", q, 3, dz), dev(1, 0, 0))
        wire.send(at(0, 0, dz), at(0, 1, dz), ("x", q, 1, dz), dev(3, 0, 0))

    def stage_b(q, near):
        _, at = view(q)
        wire.arrive(at(0, 0, near), ("z", q, near), here)
        if near == pair(q)[0]:
            wire.send(at(0, 0, near), at(0, 0, 2), ("z", q, 2), dev(0, 4 - near, 0))
        along_x(q, near)

    def stage_c(q):
        _, at = view(q)
        wire.arrive(at(0, 0, 2), ("z", q, 2), here)
        along_x(q, 2)
        local[q].wait()
        wire.send(at(0, 0), at(1, 0), ("c", q, 0), here)

    def stage_d(q, dz):
        _, at = view(q)
        near = pair(q)[0]
        wire.arrive(at(0, near, dz), ("x", q, near, dz), here)
        wire.send(at(0, near, dz), at(0, 2, dz), ("x", q, 2, dz), dev(4 - near, 0, 0))

    def stage_h(q):
        _, at = view(q)
        plain = pair(q)[1]
        for dz in range(4):
            wire.arrive(at(0, plain, dz), ("x", q, plain, dz), here)
        wire.send(at(0, plain), at(1, plain), ("c", q, plain), here)

    def stage_i(q):
        _, at = view(q)
        near = pair(q)[0]
        wire.send(at(0, near), at(1, near), ("c", q, near), here)

    def stage_e(q):
        _, at = view(q)
        for dz in range(4):
            wire.arrive(at(0, 2, dz), ("x", q, 2, dz), here)
        wire.send(at(0, 2), at(1, 2), ("c", q, 2), here)

    def stage_f(q):
        _, at = view(q)
        for dx in range(4):
            wire.arrive(at(1, dx), ("c", q, dx), here)

    expert = me // 4
    first = (((0,), (0,)), ((), ()))

    def spread(dc, dz):
        for dx in (1, 3, 2):
            wire.arrive(acts.at[dc, 4 - dx, dz], ("acts", dc, dz, dx), here)
        for dx in range(4):
            act = held[dc, dz, x] if dx == 0 else acts[dc, dx, dz]
            slot = lax.broadcasted_iota(jnp.int32, (cap, 128), 0).astype(f32)
            hit = slot == meta[dc, dx, dz, pl.ds(expert, 1), :]
            gate = meta[dc, dx, dz, pl.ds(expert + EXPERTS, 1), :]
            pick = jnp.where(hit, 1.0, 0.0).astype(bf16)
            gate_pick = jnp.where(hit, gate, 0.0).astype(bf16)
            both = lax.dot_general(pick, act, first, preferred_element_type=f32)
            g = lax.dot_general(
                gate_pick, jnp.ones((cap, hid), bf16), first, preferred_element_type=f32
            )[:tokens]
            a = both[:tokens, :hid]
            b = both[:tokens, hid:]
            sig = jax.nn.sigmoid(a)
            silu = g * (a * sig)
            slope = g * b * sig * (1.0 + a * (1.0 - sig))
            third = (silu * b).astype(bf16)
            low = (dx * 4 + dz) * rows
            for q in range(chunks):
                mine = slice(q * rows, (q + 1) * rows)
                coef_a[q, dc, low : low + rows, :] = slope[mine]
                coef_b[q, dc, low : low + rows, :] = silu[mine]
                scaled[q, dc, low : low + rows, :] = third[mine]

    last = (((1,), (1,)), ((), ()))
    plainly = (((1,), (0,)), ((), ()))
    step = 256

    def stage_g(q, dc):
        mine = up[q, dc].reshape(16 * rows, width)
        grad_h = lax.dot_general(mine, w_down[...], last, preferred_element_type=f32)
        grad_a[...] = (grad_h * coef_a[q, dc]).astype(bf16)
        grad_b[...] = (grad_h * coef_b[q, dc]).astype(bf16)

        def body(n, carry):
            cols = pl.ds(pl.multiple_of(n * step, step), step)
            total = lax.dot_general(
                grad_a[...], w_gate[:, cols], plainly, preferred_element_type=f32
            ) + lax.dot_general(grad_b[...], w_up[:, cols], plainly, preferred_element_type=f32)
            part[q, dc, :, :, :, cols] = total.astype(bf16).reshape(4, 4, rows, step)
            return carry

        lax.fori_loop(0, width // step, body, 0)
        if dc == 1:
            wire.send(part.at[q, 1], from_core.at[q], ("back c", q), here)

    def weight_grad():
        left = scaled[...].reshape(32 * chunks * rows, hid)
        wide = 512

        def body(n, carry):
            cols = pl.ds(pl.multiple_of(n * wide, wide), wide)
            down_ref[:, cols] = lax.dot_general(
                left,
                up[:, :, :, :, :, cols].reshape(32 * chunks * rows, wide),
                (((0,), (0,)), ((), ())),
                preferred_element_type=f32,
            ).astype(bf16)
            return carry

        lax.fori_loop(0, width // wide, body, 0)

    def back_b(q, dz):
        by_way, plain = pair(q)
        if dz == 2:
            wire.arrive(from_core.at[q], ("back c", q), here)

        def body(dx, carry):
            mine = from_core.at[q, dx, dz]
            add_block(mine, [mine, part.at[q, 0, dx, dz]], 0, width)
            return carry

        lax.fori_loop(0, 4, body, 0)
        for dx, key, way in ((2, 2, by_way), (plain, 4 - plain, plain)):
            wire.send(
                from_core.at[q, dx, dz], from_x.at[q, key, dz], ("back x", q, key, dz), dev(way, 0, 0)
            )

    def back_c(q, dz):
        by_way, _ = pair(q)
        mine = from_core.at[q, by_way, dz]
        wire.arrive(from_x.at[q, 2, dz], ("back x", q, 2, dz), here)
        add_block(mine, [mine, from_x.at[q, 2, dz]], 0, width)
        key = 4 - by_way
        wire.send(mine, from_x.at[q, key, dz], ("back x", q, key, dz), dev(by_way, 0, 0))

    half = width // 2

    def half_of(ref, h):
        return ref.at[:, pl.ds(h * half, half)]

    def give_z(q, dz, key, way, h):
        wire.send(
            half_of(from_core.at[q, 0, dz], h),
            half_of(from_z.at[q, key], h),
            ("back z", q, key, h),
            dev(0, way, 0),
        )

    def back_d(q, dz):
        by_way, plain = pair(q)
        mine = from_core.at[q, 0, dz]
        for dx in (1, 3):
            wire.arrive(from_x.at[q, dx, dz], ("back x", q, dx, dz), here)
        add_block(mine, [mine, from_x.at[q, 1, dz], from_x.at[q, 3, dz]], 0, width)
        for h in (0, 1):
            if dz == 2:
                give_z(q, 2, 2, by_way, h)
            if dz == plain:
                give_z(q, plain, 4 - plain, plain, h)

    def back_e(q, h):
        by_way, _ = pair(q)
        mine = from_core.at[q, 0, by_way]
        wire.arrive(half_of(from_z.at[q, 2], h), ("back z", q, 2, h), here)
        add_block(mine, [mine, from_z.at[q, 2]], h * half, half)
        give_z(q, by_way, 4 - by_way, by_way, h)

    def back_f(q, h):
        mine = from_core.at[q, 0, 0]
        for dz in (1, 3):
            wire.arrive(half_of(from_z.at[q, dz], h), ("back z", q, dz, h), here)
        add_block(mine, [mine, from_z.at[q, 1], from_z.at[q, 3]], h * half, half)
        wire.send(half_of(mine, h), half_of(landed.at[q], h), ("s", q, h), before)

    def meta_near():
        stage_b(-1, 1)
        stage_b(-1, 3)

    def meta_rest():
        stage_c(-1)
        for dz in range(4):
            stage_d(-1, dz)
        stage_h(-1)
        stage_i(-1)
        stage_e(-1)
        stage_f(-1)
        for key in ("w_down", "w_gate", "w_up"):
            local[key].wait()

    meta_own()
    stage_a(-1)
    plan = (
        "A0 A1 M0 S",
        "X00 X10 D00 D10",
        "B03 B01 A2 D03",
        "D01 B11 B13 A3",
        "D20 D11 D13 D30",
        "X03 X01 M1 P00",
        "P10 P03 P01 X13",
        "X11 P13 P11 X12",
        "X02 P12 P02 B23",
        "C0 D23 D02 I0",
        "H0 C1 B21 E0",
        "D12 I1 H1 F0",
        "G0 D21 B33 B31",
        "g0 E1 b02 b03",
        "F1 D33 G1 C2",
        "D31 c02 g1 c03",
        "b01 b00 b12 b11",
        "D22 I2 H2 C3",
        "b13 b10 d02 d03",
        "c12 c01 c11 c00",
        "E2 H3 F2 G2",
        "g2 c13 c10 D32",
        "I3 d12 b22 b23",
        "d11 b21 b20 d01",
        "e01 d13 e00 d00",
        "d10 E3 c22 F3",
        "G3 c23 e10 g3",
        "c21 e11 c20 b32",
        "d22 b31 b33 d23",
        "b30 W c32 f10",
        "d20 f01 f00 c31",
        "d21 f11 c33 c30",
        "e20 d32 d31 e21",
        "d33 d30 f20 e30",
        "e31 f30 f21 f31",
    )
    table = {
        "A": stage_a, "B": stage_b, "C": stage_c, "D": stage_d, "E": stage_e, "F": stage_f,
        "H": stage_h, "I": stage_i, "X": slots_x, "P": spread, "S": slots_start,
        "G": lambda q: stage_g(q, 1), "g": lambda q: stage_g(q, 0), "W": weight_grad,
        "b": back_b, "c": back_c, "d": back_d, "e": back_e, "f": back_f,
        "M": lambda late: meta_rest() if late else meta_near(),
    }
    for line in plan:
        for entry in line.split():
            table[entry[0]](*[int(digit) for digit in entry[1:]])
    for q in range(chunks):
        for h in (0, 1):
            wire.arrive(half_of(landed.at[q], h), ("s", q, h), here)
        out_ref[q] = landed[q]
    wire.drain()


def store_kernel(grad_in_ref, grad_down_ref, out_ref, down_ref):
    out_ref[...] = grad_in_ref[...]
    down_ref[...] = grad_down_ref[...]


def on_device(grad_out, pre_act, route_ids, route_gate, w_gate, w_up, w_down):
    tokens = grad_out.shape[1]
    width = grad_out.shape[2]
    hid = w_down.shape[1]
    cap = 3 * tokens // 8
    chunks = tokens // ROWS
    bf16 = jnp.bfloat16
    f32 = jnp.float32
    saved = pre_act[0].transpose(1, 0, 2, 3).reshape(tokens * 2, -1)
    up = grad_out[0].reshape(chunks, ROWS, width)

    vm = pl.BlockSpec(memory_space=VMEM)
    anywhere = pl.BlockSpec(memory_space=pl.ANY)
    dma = pltpu.SemaphoreType.DMA
    block = (ROWS, width)
    copies = 31 + 19 * (chunks + 1) + 21 * chunks
    grad_in, grad_down = pl.pallas_call(
        layer_kernel,
        out_shape=(
            jax.ShapeDtypeStruct((chunks,) + block, bf16),
            jax.ShapeDtypeStruct((hid, width), bf16),
        ),
        in_specs=[vm] * 4 + [anywhere] * 3,
        out_specs=(vm, vm),
        scratch_shapes=[
            VMEM((chunks, 2, 4, 4) + block, bf16),
            VMEM((2, 4, 4, 2 * EXPERTS, 128), f32),
            VMEM((2 * EXPERTS, 128), f32),
            VMEM((4, 4, 2, cap, 2 * hid), bf16),
            VMEM((2, 4, 4, cap, 2 * hid), bf16),
            VMEM((2, 4, 4, cap, 2 * hid), bf16),
            VMEM((hid, width), bf16),
            VMEM((hid, width), bf16),
            VMEM((hid, width), bf16),
            VMEM((chunks, 2, 16 * ROWS, hid), f32),
            VMEM((chunks, 2, 16 * ROWS, hid), f32),
            VMEM((chunks, 2, 16 * ROWS, hid), bf16),
            VMEM((16 * ROWS, hid), bf16),
            VMEM((16 * ROWS, hid), bf16),
            VMEM((chunks, 2, 4, 4) + block, bf16),
            VMEM((chunks, 4, 4) + block, bf16),
            VMEM((chunks, 4, 4) + block, bf16),
            VMEM((chunks, 4) + block, bf16),
            VMEM((chunks,) + block, bf16),
            dma((copies,)),
            dma((copies,)),
            dma((chunks + 6,)),
        ],
        compiler_params=pltpu.CompilerParams(
            collective_id=0, has_side_effects=True, vmem_limit_bytes=60 << 20
        ),
        name="layer",
    )(up, saved, route_ids[0].T, route_gate[0].T, w_gate[0].T, w_up[0].T, w_down[0])
    grad_in = grad_in.reshape(tokens, width)
    return tuple(
        out[None]
        for out in pl.pallas_call(
            store_kernel,
            out_shape=(
                jax.ShapeDtypeStruct(grad_in.shape, bf16),
                jax.ShapeDtypeStruct(grad_down.shape, bf16),
            ),
            in_specs=[vm] * 2,
            out_specs=(vm, vm),
            name="store",
        )(grad_in, grad_down)
    )


def solution(mesh):
    tok = P("section", "expert", None)
    return jax.shard_map(
        on_device,
        mesh=mesh,
        in_specs=(
            tok,
            P("section", "expert", None, None, None),
            tok,
            tok,
            P("section", None, "expert"),
            P("section", None, "expert"),
            tok,
        ),
        out_specs=(tok, tok),
        check_vma=False,
    )
```

```python
import functools

import jax
import jax.numpy as jnp
from jax import lax
from jax.experimental import pallas as pl
from jax.experimental.pallas import tpu as pltpu
from jax.sharding import PartitionSpec as P

EXPERTS = 8
ROWS = 16
MESH = pl.DeviceIdType.MESH
VMEM = pltpu.VMEM


class Wire:
    def __init__(self, send_sems, recv_sems):
        self.send_sems = send_sems
        self.recv_sems = recv_sems
        self.sent = []
        self.used = {}

    def recv_sem(self, key):
        if key not in self.used:
            self.used[key] = len(self.used)
        return self.recv_sems.at[self.used[key]]

    def send(self, src, dst, key, device):
        copy = pltpu.make_async_remote_copy(
            src_ref=src,
            dst_ref=dst,
            send_sem=self.send_sems.at[len(self.sent)],
            recv_sem=self.recv_sem(key),
            device_id=device,
            device_id_type=MESH,
        )
        copy.start()
        self.sent.append(copy)

    def arrive(self, dst, key, device):
        pltpu.make_async_remote_copy(
            src_ref=dst,
            dst_ref=dst,
            send_sem=self.send_sems.at[0],
            recv_sem=self.recv_sem(key),
            device_id=device,
            device_id_type=MESH,
        ).wait_recv()

    def drain(self):
        for copy in self.sent:
            copy.wait_send()


def place():
    me = lax.axis_index("expert")
    x = me // 8
    z = lax.rem(me // 2, 4)
    c = lax.rem(me, 2)

    def dev(dx, dz, dc):
        core = c if dc == 0 else 1 - c
        return {"expert": lax.rem(x + dx, 4) * 8 + lax.rem(z + dz, 4) * 2 + core}

    return x, z, c, dev


def greet(devices):
    for device in devices:
        pl.semaphore_signal(
            pltpu.get_barrier_semaphore(), inc=1, device_id=device, device_id_type=MESH
        )


def add_block(dst, terms, low, size):
    part = min(size, 1024)
    for at in range(low, low + size, part):
        cols = pl.ds(at, part)
        total = terms[0][:, cols].astype(jnp.float32)
        for term in terms[1:]:
            total = total + term[:, cols].astype(jnp.float32)
        dst[:, cols] = total.astype(jnp.bfloat16)


def layer_kernel(
    up_ref, saved_ref, route_ref, gate_ref, w_gate_ref, w_up_ref, w_down_ref, out_ref, down_ref,
    up, meta, own_meta, slots, held, acts, w_gate, w_up, w_down, coef_a, coef_b, scaled, grad_a, grad_b,
    down, part, from_core, from_x, from_z, landed, send_sems, recv_sems, copy_sems,
):
    x, z, c, dev = place()
    count = lax.axis_size("section")
    section = lax.axis_index("section")
    me = lax.axis_index("expert")
    before = {"section": lax.rem(section + count - 1, count), "expert": me}
    after = {"section": lax.rem(section + 1, count), "expert": me}
    here = dev(0, 0, 1)
    chunks, rows, width = up_ref.shape
    hid = w_down_ref.shape[0]
    cap = acts.shape[3]
    tokens = chunks * rows
    bf16 = jnp.bfloat16
    f32 = jnp.float32
    wire = Wire(send_sems, recv_sems)
    local = {}

    def keep(key, src, dst):
        copy = pltpu.make_async_copy(src, dst, copy_sems.at[len(local)])
        copy.start()
        local[key] = copy

    partners = [dev(0, dz, dc) for dz in (1, 2, 3) for dc in (0, 1)]
    partners += [dev(1, 0, 0), dev(2, 0, 0), dev(3, 0, 0), here, before, after]
    greet(partners)
    keep("w_down", w_down_ref, w_down)
    keep("w_gate", w_gate_ref, w_gate)
    keep("w_up", w_up_ref, w_up)
    core = (c, 1 - c)

    lane = lax.broadcasted_iota(jnp.int32, (EXPERTS, 2 * tokens), 1)
    hit = lane * 0 + jnp.concatenate([route_ref[0:1, :], route_ref[1:2, :]], axis=1)
    hit = hit == lax.broadcasted_iota(jnp.int32, (EXPERTS, 2 * tokens), 0)

    def routes():
        earlier = lax.broadcasted_iota(jnp.int32, (2 * tokens, 2 * tokens), 0) % tokens
        later = lax.broadcasted_iota(jnp.int32, (2 * tokens, 2 * tokens), 1) % tokens
        upto = jnp.where(earlier <= later, 1.0, 0.0).astype(bf16)
        ones = jnp.where(hit, 1.0, 0.0).astype(bf16)
        rank = jnp.dot(ones, upto, preferred_element_type=f32) - 1.0
        return jnp.where(hit, rank, -1.0)

    rank = routes()

    def meta_own():
        gates = gate_ref[...].astype(f32)
        gates = jnp.concatenate([gates[0:1, :], gates[1:2, :]], axis=1)
        gates = jnp.where(hit, jnp.broadcast_to(gates, hit.shape), 0.0)
        either = jnp.maximum(rank, pltpu.roll(rank, tokens, 1))
        own_meta[0:EXPERTS, :] = jnp.where(lane < tokens, either, -1.0)
        own_meta[EXPERTS:, :] = gates + pltpu.roll(gates, tokens, 1)

    def slots_fill():
        slot = lax.broadcasted_iota(jnp.int32, (cap, 2 * tokens), 0).astype(f32)
        picks = [
            jnp.where(slot == rank[e : e + 1, :], 1.0, 0.0) for e in range(EXPERTS)
        ]
        pick = jnp.concatenate(picks, axis=0).astype(bf16)
        side = 4 * hid
        for low in (0, side):
            j = low // side
            taken = jnp.dot(
                pick,
                jnp.concatenate([saved_ref[:, k, j, :] for k in (0, 1)], axis=0),
                preferred_element_type=f32,
            )
            for e in range(EXPERTS):
                for m in range(4):
                    piece = taken[e * cap : (e + 1) * cap, m * hid : (m + 1) * hid]
                    at = 0 if low == 0 else hid
                    slots[e // 2, 2 * (e % 2) + m // 2, m % 2, :, at : at + hid] = piece.astype(bf16)

    def slots_start():
        for dz in (1, 3, 2):
            for dc in (0, 1):
                wire.send(
                    slots.at[:, lax.rem(z + dz, 4), core[dc]],
                    held.at[dc, 4 - dz],
                    ("held", dc, 4 - dz),
                    dev(0, dz, dc),
                )
        wire.send(slots.at[:, z, core[1]], held.at[1, 0], ("held", 1, 0), here)
        keep("slots", slots.at[:, z, c], held.at[0, 0])

    def slots_x(dc, dz):
        if (dc, dz) == (0, 0):
            local["slots"].wait()
        else:
            wire.arrive(held.at[dc, dz], ("held", dc, dz), here)
        for dx in (2, 1, 3):
            wire.send(
                held.at[dc, dz, lax.rem(x + dx, 4)],
                acts.at[dc, 4 - dx, dz],
                ("acts", dc, dz, dx),
                dev(dx, 0, 0),
            )

    def view(q):
        if q < 0:
            return own_meta, lambda dc, dx, *dz: meta.at[(dc, dx) + dz]
        return up_ref.at[q], lambda dc, dx, *dz: up.at[(q, dc, dx) + dz]

    def pair(q):
        return (1, 3) if q % 2 == 0 else (3, 1)

    def stage_a(q):
        mine, at = view(q)
        wire.send(mine, at(0, 0, 3), ("z", q, 3), dev(0, 1, 0))
        wire.send(mine, at(0, 0, 1), ("z", q, 1), dev(0, 3, 0))
        wire.send(mine, at(0, 3, 0), ("x", q, 3, 0), dev(1, 0, 0))
        wire.send(mine, at(0, 1, 0), ("x", q, 1, 0), dev(3, 0, 0))
        keep(q, mine, at(0, 0, 0))

    def along_x(q, dz):
        _, at = view(q)
        wire.send(at(0, 0, dz), at(0, 3, dz), ("x", q, 3, dz), dev(1, 0, 0))
        wire.send(at(0, 0, dz), at(0, 1, dz), ("x", q, 1, dz), dev(3, 0, 0))

    def stage_b(q, near):
        _, at = view(q)
        wire.arrive(at(0, 0, near), ("z", q, near), here)
        if near == pair(q)[0]:
            wire.send(at(0, 0, near), at(0, 0, 2), ("z", q, 2), dev(0, 4 - near, 0))
        along_x(q, near)

    def stage_c(q):
        _, at = view(q)
        wire.arrive(at(0, 0, 2), ("z", q, 2), here)
        along_x(q, 2)
        local[q].wait()
        wire.send(at(0, 0), at(1, 0), ("c", q, 0), here)

    def stage_d(q, dz):
        _, at = view(q)
        near = pair(q)[0]
        wire.arrive(at(0, near, dz), ("x", q, near, dz), here)
        wire.send(at(0, near, dz), at(0, 2, dz), ("x", q, 2, dz), dev(4 - near, 0, 0))

    def stage_h(q):
        _, at = view(q)
        plain = pair(q)[1]
        for dz in range(4):
            wire.arrive(at(0, plain, dz), ("x", q, plain, dz), here)
        wire.send(at(0, plain), at(1, plain), ("c", q, plain), here)

    def stage_i(q):
        _, at = view(q)
        near = pair(q)[0]
        wire.send(at(0, near), at(1, near), ("c", q, near), here)

    def stage_e(q):
        _, at = view(q)
        for dz in range(4):
            wire.arrive(at(0, 2, dz), ("x", q, 2, dz), here)
        wire.send(at(0, 2), at(1, 2), ("c", q, 2), here)

    def stage_f(q):
        _, at = view(q)
        for dx in range(4):
            wire.arrive(at(1, dx), ("c", q, dx), here)

    expert = me // 4
    first = (((0,), (0,)), ((), ()))

    def spread(dc, dz):
        for dx in (1, 3, 2):
            wire.arrive(acts.at[dc, 4 - dx, dz], ("acts", dc, dz, dx), here)
        for dx in range(4):
            act = held[dc, dz, x] if dx == 0 else acts[dc, dx, dz]
            slot = lax.broadcasted_iota(jnp.int32, (cap, 128), 0).astype(f32)
            hit = slot == meta[dc, dx, dz, pl.ds(expert, 1), :]
            gate = meta[dc, dx, dz, pl.ds(expert + EXPERTS, 1), :]
            pick = jnp.where(hit, 1.0, 0.0).astype(bf16)
            gate_pick = jnp.where(hit, gate, 0.0).astype(bf16)
            both = lax.dot_general(pick, act, first, preferred_element_type=f32)
            g = lax.dot_general(
                gate_pick, jnp.ones((cap, hid), bf16), first, preferred_element_type=f32
            )[:tokens]
            a = both[:tokens, :hid]
            b = both[:tokens, hid:]
            sig = jax.nn.sigmoid(a)
            silu = g * (a * sig)
            slope = g * b * sig * (1.0 + a * (1.0 - sig))
            third = (silu * b).astype(bf16)
            low = (dx * 4 + dz) * rows
            for q in range(chunks):
                mine = slice(q * rows, (q + 1) * rows)
                coef_a[q, dc, low : low + rows, :] = slope[mine]
                coef_b[q, dc, low : low + rows, :] = silu[mine]
                scaled[q, dc, low : low + rows, :] = third[mine]

    last = (((1,), (1,)), ((), ()))
    plainly = (((1,), (0,)), ((), ()))
    step = 256

    half = width // 2

    def stage_g(q, dc, h):
        if h == 0:
            mine = up[q, dc].reshape(16 * rows, width)
            grad_h = lax.dot_general(mine, w_down[...], last, preferred_element_type=f32)
            grad_a[q, dc] = (grad_h * coef_a[q, dc]).astype(bf16)
            grad_b[q, dc] = (grad_h * coef_b[q, dc]).astype(bf16)

        def body(n, carry):
            cols = pl.ds(pl.multiple_of(h * half + n * step, step), step)
            total = lax.dot_general(
                grad_a[q, dc], w_gate[:, cols], plainly, preferred_element_type=f32
            ) + lax.dot_general(grad_b[q, dc], w_up[:, cols], plainly, preferred_element_type=f32)
            part[q, dc, :, :, :, cols] = total.astype(bf16).reshape(4, 4, rows, step)
            return carry

        lax.fori_loop(0, half // step, body, 0)
        if dc == 1:
            cols = pl.ds(h * half, half)
            wire.send(
                part.at[q, 1, :, :, :, cols],
                from_core.at[q, :, :, :, cols],
                ("back c", q, h),
                here,
            )

    def weight_grad():
        left = scaled[...].reshape(32 * chunks * rows, hid)
        wide = 512

        def body(n, carry):
            cols = pl.ds(pl.multiple_of(n * wide, wide), wide)
            down[:, cols] = lax.dot_general(
                left,
                up[:, :, :, :, :, cols].reshape(32 * chunks * rows, wide),
                (((0,), (0,)), ((), ())),
                preferred_element_type=f32,
            ).astype(bf16)
            return carry

        lax.fori_loop(0, width // wide, body, 0)
        keep("down", down, down_ref)

    def half_of(ref, h):
        return ref.at[:, pl.ds(h * half, half)]

    def give_x(q, dx, dz, key, way, h):
        wire.send(
            half_of(from_core.at[q, dx, dz], h),
            half_of(from_x.at[q, key, dz], h),
            ("back x", q, key, dz, h),
            dev(way, 0, 0),
        )

    def give_z(q, dz, key, way, h):
        wire.send(
            half_of(from_core.at[q, 0, dz], h),
            half_of(from_z.at[q, key], h),
            ("back z", q, key, h),
            dev(0, way, 0),
        )

    def back_b(q, dz, h):
        by_way, plain = pair(q)
        if dz == 2:
            cols = pl.ds(h * half, half)
            wire.arrive(from_core.at[q, :, :, :, cols], ("back c", q, h), here)

        def body(dx, carry):
            mine = from_core.at[q, dx, dz]
            add_block(mine, [mine, part.at[q, 0, dx, dz]], h * half, half)
            return carry

        lax.fori_loop(0, 4, body, 0)
        give_x(q, 2, dz, 2, by_way, h)
        give_x(q, plain, dz, 4 - plain, plain, h)

    def back_c(q, dz, h):
        by_way, _ = pair(q)
        mine = from_core.at[q, by_way, dz]
        wire.arrive(half_of(from_x.at[q, 2, dz], h), ("back x", q, 2, dz, h), here)
        add_block(mine, [mine, from_x.at[q, 2, dz]], h * half, half)
        give_x(q, by_way, dz, 4 - by_way, by_way, h)

    def back_d(q, dz, h):
        by_way, plain = pair(q)
        mine = from_core.at[q, 0, dz]
        for dx in (1, 3):
            wire.arrive(half_of(from_x.at[q, dx, dz], h), ("back x", q, dx, dz, h), here)
        add_block(mine, [mine, from_x.at[q, 1, dz], from_x.at[q, 3, dz]], h * half, half)
        if dz == 2:
            give_z(q, 2, 2, by_way, h)
        if dz == plain:
            give_z(q, plain, 4 - plain, plain, h)

    def back_e(q, h):
        by_way, _ = pair(q)
        mine = from_core.at[q, 0, by_way]
        wire.arrive(half_of(from_z.at[q, 2], h), ("back z", q, 2, h), here)
        add_block(mine, [mine, from_z.at[q, 2]], h * half, half)
        give_z(q, by_way, 4 - by_way, by_way, h)

    def back_f(q, h):
        mine = from_core.at[q, 0, 0]
        for dz in (1, 3):
            wire.arrive(half_of(from_z.at[q, dz], h), ("back z", q, dz, h), here)
        add_block(mine, [mine, from_z.at[q, 1], from_z.at[q, 3]], h * half, half)
        wire.send(half_of(mine, h), half_of(landed.at[q], h), ("s", q, h), before)

    def meta_near():
        stage_b(-1, 1)
        stage_b(-1, 3)

    def meta_rest():
        stage_c(-1)
        for dz in range(4):
            stage_d(-1, dz)
        stage_h(-1)
        stage_i(-1)
        stage_e(-1)
        stage_f(-1)
        for key in ("w_down", "w_gate", "w_up"):
            local[key].wait()

    def theirs(q, h):
        stage_g(q, 1, h)

    def ours(q, h):
        stage_g(q, 0, h)

    meta_own()
    slots_fill()
    pl.semaphore_wait(pltpu.get_barrier_semaphore(), len(partners))
    stage_a(-1)
    steps = (
        (stage_a, 0), (meta_near,), (slots_start,), (slots_x, 0, 0), (slots_x, 1, 0),
        (stage_d, 0, 0), (stage_b, 0, 1), (stage_b, 0, 3), (stage_a, 1), (stage_a, 2),
        (stage_d, 0, 1), (stage_d, 0, 3), (stage_d, 1, 0), (slots_x, 0, 3), (slots_x, 0, 1),
        (stage_d, 2, 0), (slots_x, 1, 3), (slots_x, 1, 1), (meta_rest,), (spread, 0, 1),
        (spread, 1, 3), (spread, 0, 3), (spread, 0, 0), (spread, 1, 0), (spread, 1, 1),
        (slots_x, 0, 2), (slots_x, 1, 2), (spread, 0, 2), (spread, 1, 2), (stage_c, 0),
        (stage_b, 1, 3), (stage_a, 3), (stage_d, 0, 2), (stage_h, 0), (stage_i, 0),
        (stage_d, 1, 3), (stage_b, 2, 3), (stage_b, 1, 1), (stage_d, 3, 0), (stage_e, 0),
        (stage_d, 2, 3), (stage_f, 0), (theirs, 0, 0), (theirs, 0, 1), (stage_d, 1, 1),
        (ours, 0, 0), (stage_c, 1), (stage_b, 2, 1), (ours, 0, 1), (back_b, 0, 2, 0),
        (back_b, 0, 2, 1), (back_b, 0, 3, 1), (back_b, 0, 1, 1), (back_b, 0, 0, 1), (back_b, 0, 3, 0),
        (back_b, 0, 1, 0), (back_b, 0, 0, 0), (stage_h, 1), (stage_d, 1, 2), (stage_i, 1),
        (stage_b, 3, 3), (stage_d, 2, 1), (stage_b, 3, 1), (back_c, 0, 2, 0), (back_c, 0, 2, 1),
        (back_c, 0, 3, 1), (back_c, 0, 1, 1), (back_c, 0, 0, 1), (back_c, 0, 3, 0), (back_c, 0, 1, 0),
        (stage_c, 2), (back_c, 0, 0, 0), (stage_e, 1), (stage_d, 3, 3), (stage_f, 1),
        (theirs, 1, 0), (stage_d, 3, 1), (stage_c, 3), (theirs, 1, 1), (back_d, 0, 2, 0),
        (ours, 1, 0), (back_d, 0, 3, 1), (back_b, 1, 2, 0), (stage_d, 2, 2), (back_b, 1, 1, 0),
        (ours, 1, 1), (stage_h, 3), (back_b, 1, 2, 1), (back_d, 0, 3, 0), (back_d, 0, 0, 1),
        (back_b, 1, 1, 1), (back_b, 1, 3, 1), (back_d, 0, 1, 0), (stage_i, 2), (back_d, 0, 1, 1),
        (back_c, 1, 2, 0), (back_d, 0, 2, 1), (back_b, 1, 0, 1), (back_b, 1, 3, 0), (back_b, 1, 0, 0),
        (stage_h, 2), (stage_e, 2), (back_d, 0, 0, 0), (back_c, 1, 1, 0), (back_e, 0, 0),
        (back_c, 1, 2, 1), (stage_f, 2), (theirs, 2, 0), (back_c, 1, 3, 1), (theirs, 2, 1),
        (ours, 2, 0), (back_c, 1, 3, 0), (stage_d, 3, 2), (stage_i, 3), (back_e, 0, 1),
        (back_d, 1, 2, 0), (ours, 2, 1), (back_c, 1, 0, 1), (back_b, 2, 2, 0), (back_c, 1, 0, 0),
        (back_b, 2, 3, 0), (back_c, 1, 1, 1), (back_b, 2, 2, 1), (back_d, 1, 2, 1), (back_b, 2, 3, 1),
        (back_b, 2, 1, 1), (back_f, 0, 0), (back_d, 1, 3, 1), (back_b, 2, 0, 1), (back_b, 2, 1, 0),
        (back_b, 2, 0, 0), (back_d, 1, 0, 1), (back_d, 1, 1, 0), (back_d, 1, 3, 0), (back_d, 1, 0, 0),
        (stage_e, 3), (back_d, 1, 1, 1), (back_f, 0, 1), (back_e, 1, 0), (back_c, 2, 2, 0),
        (back_c, 2, 3, 0), (stage_f, 3), (theirs, 3, 0), (back_c, 2, 2, 1), (back_c, 2, 3, 1),
        (theirs, 3, 1), (back_e, 1, 1), (ours, 3, 0), (back_c, 2, 0, 1), (back_c, 2, 1, 0),
        (back_b, 3, 2, 0), (back_b, 3, 1, 0), (back_c, 2, 0, 0), (ours, 3, 1), (back_b, 3, 2, 1),
        (back_d, 2, 2, 0), (back_d, 2, 3, 0), (back_b, 3, 1, 1), (back_b, 3, 3, 1), (back_b, 3, 0, 1),
        (back_d, 2, 2, 1), (back_f, 1, 0), (back_c, 3, 2, 0), (back_b, 3, 3, 0), (back_b, 3, 0, 0),
        (back_c, 3, 1, 0), (back_d, 2, 3, 1), (weight_grad,), (back_c, 3, 2, 1), (back_d, 3, 2, 0),
        (back_c, 3, 0, 1), (back_d, 2, 0, 1), (back_d, 2, 1, 0), (back_c, 3, 3, 0), (back_c, 3, 1, 1),
        (back_c, 3, 3, 1), (back_f, 1, 1), (back_c, 2, 1, 1), (back_e, 2, 0), (back_c, 3, 0, 0),
        (back_d, 2, 0, 0), (back_d, 3, 1, 0), (back_d, 3, 2, 1), (back_d, 3, 0, 1), (back_d, 3, 3, 0),
        (back_d, 2, 1, 1), (back_e, 2, 1), (back_d, 3, 1, 1), (back_d, 3, 3, 1), (back_d, 3, 0, 0),
        (back_e, 3, 0), (back_f, 2, 0), (back_e, 3, 1), (back_f, 2, 1), (back_f, 3, 0),
        (back_f, 3, 1),
    )
    for stage, *at in steps:
        stage(*at)
    for q in range(chunks):
        for h in (0, 1):
            wire.arrive(half_of(landed.at[q], h), ("s", q, h), here)
        keep(("out", q), landed.at[q], out_ref.at[q])
    local["down"].wait()
    for q in range(chunks):
        local["out", q].wait()
    wire.drain()


def store_kernel(grad_in_ref, grad_down_ref, out_ref, down_ref):
    out_ref[...] = grad_in_ref[...]
    down_ref[...] = grad_down_ref[...]


def on_device(grad_out, pre_act, route_ids, route_gate, w_gate, w_up, w_down):
    tokens = grad_out.shape[1]
    width = grad_out.shape[2]
    hid = w_down.shape[1]
    cap = 3 * tokens // 8
    chunks = tokens // ROWS
    bf16 = jnp.bfloat16
    f32 = jnp.float32
    saved = pre_act[0]
    up = grad_out[0].reshape(chunks, ROWS, width)

    vm = pl.BlockSpec(memory_space=VMEM)
    anywhere = pl.BlockSpec(memory_space=pl.ANY)
    dma = pltpu.SemaphoreType.DMA
    block = (ROWS, width)
    copies = 31 + 19 * (chunks + 1) + 34 * chunks
    grad_in, grad_down = pl.pallas_call(
        layer_kernel,
        out_shape=(
            jax.ShapeDtypeStruct((chunks,) + block, bf16),
            jax.ShapeDtypeStruct((hid, width), bf16),
        ),
        in_specs=[vm] * 4 + [anywhere] * 3,
        out_specs=(anywhere, anywhere),
        scratch_shapes=[
            VMEM((chunks, 2, 4, 4) + block, bf16),
            VMEM((2, 4, 4, 2 * EXPERTS, 128), f32),
            VMEM((2 * EXPERTS, 128), f32),
            VMEM((4, 4, 2, cap, 2 * hid), bf16),
            VMEM((2, 4, 4, cap, 2 * hid), bf16),
            VMEM((2, 4, 4, cap, 2 * hid), bf16),
            VMEM((hid, width), bf16),
            VMEM((hid, width), bf16),
            VMEM((hid, width), bf16),
            VMEM((chunks, 2, 16 * ROWS, hid), f32),
            VMEM((chunks, 2, 16 * ROWS, hid), f32),
            VMEM((chunks, 2, 16 * ROWS, hid), bf16),
            VMEM((chunks, 2, 16 * ROWS, hid), bf16),
            VMEM((chunks, 2, 16 * ROWS, hid), bf16),
            VMEM((hid, width), bf16),
            VMEM((chunks, 2, 4, 4) + block, bf16),
            VMEM((chunks, 4, 4) + block, bf16),
            VMEM((chunks, 4, 4) + block, bf16),
            VMEM((chunks, 4) + block, bf16),
            VMEM((chunks,) + block, bf16),
            dma((copies,)),
            dma((copies,)),
            dma((2 * chunks + 6,)),
        ],
        compiler_params=pltpu.CompilerParams(
            collective_id=0, has_side_effects=True, vmem_limit_bytes=60 << 20
        ),
        name="layer",
    )(up, saved, route_ids[0].T, route_gate[0].T, w_gate[0].T, w_up[0].T, w_down[0])
    grad_in = grad_in.reshape(tokens, width)
    return tuple(
        out[None]
        for out in pl.pallas_call(
            store_kernel,
            out_shape=(
                jax.ShapeDtypeStruct(grad_in.shape, bf16),
                jax.ShapeDtypeStruct(grad_down.shape, bf16),
            ),
            in_specs=[vm] * 2,
            out_specs=(vm, vm),
            name="store",
        )(grad_in, grad_down)
    )


def solution(mesh):
    tok = P("section", "expert", None)
    return jax.shard_map(
        on_device,
        mesh=mesh,
        in_specs=(
            tok,
            P("section", "expert", None, None, None),
            tok,
            tok,
            P("section", None, "expert"),
            P("section", None, "expert"),
            tok,
        ),
        out_specs=(tok, tok),
        check_vma=False,
    )
```

```python
import functools

import jax
import jax.numpy as jnp
from jax import lax
from jax.experimental import pallas as pl
from jax.experimental.pallas import tpu as pltpu
from jax.sharding import PartitionSpec as P

EXPERTS = 8
ROWS = 16
MESH = pl.DeviceIdType.MESH
VMEM = pltpu.VMEM


class Wire:
    def __init__(self, send_sems, recv_sems):
        self.send_sems = send_sems
        self.recv_sems = recv_sems
        self.sent = []
        self.used = {}

    def recv_sem(self, key):
        if key not in self.used:
            self.used[key] = len(self.used)
        return self.recv_sems.at[self.used[key]]

    def send(self, src, dst, key, device):
        copy = pltpu.make_async_remote_copy(
            src_ref=src,
            dst_ref=dst,
            send_sem=self.send_sems.at[len(self.sent)],
            recv_sem=self.recv_sem(key),
            device_id=device,
            device_id_type=MESH,
        )
        copy.start()
        self.sent.append(copy)

    def arrive(self, dst, key, device):
        pltpu.make_async_remote_copy(
            src_ref=dst,
            dst_ref=dst,
            send_sem=self.send_sems.at[0],
            recv_sem=self.recv_sem(key),
            device_id=device,
            device_id_type=MESH,
        ).wait_recv()

    def drain(self):
        for copy in self.sent:
            copy.wait_send()


def place():
    me = lax.axis_index("expert")
    x = me // 8
    z = lax.rem(me // 2, 4)
    c = lax.rem(me, 2)

    def dev(dx, dz, dc):
        core = c if dc == 0 else 1 - c
        return {"expert": lax.rem(x + dx, 4) * 8 + lax.rem(z + dz, 4) * 2 + core}

    return x, z, c, dev


def greet(devices):
    for device in devices:
        pl.semaphore_signal(
            pltpu.get_barrier_semaphore(), inc=1, device_id=device, device_id_type=MESH
        )


def add_block(dst, terms, low, size):
    part = min(size, 1024)
    for at in range(low, low + size, part):
        cols = pl.ds(at, part)
        total = terms[0][:, cols].astype(jnp.float32)
        for term in terms[1:]:
            total = total + term[:, cols].astype(jnp.float32)
        dst[:, cols] = total.astype(jnp.bfloat16)


def layer_kernel(
    up_ref, saved_ref, route_ref, gate_ref, w_gate_ref, w_up_ref, w_down_ref, out_ref, down_ref,
    up, meta, own_meta, slots, held, acts, w_gate, w_up, w_down, coef_a, coef_b, scaled, grad_a, grad_b,
    down, part, from_core, from_x, from_z, landed, send_sems, recv_sems, copy_sems,
):
    x, z, c, dev = place()
    count = lax.axis_size("section")
    section = lax.axis_index("section")
    me = lax.axis_index("expert")
    before = {"section": lax.rem(section + count - 1, count), "expert": me}
    after = {"section": lax.rem(section + 1, count), "expert": me}
    here = dev(0, 0, 1)
    chunks, rows, width = up_ref.shape
    hid = w_down_ref.shape[0]
    cap = acts.shape[3]
    tokens = chunks * rows
    bf16 = jnp.bfloat16
    f32 = jnp.float32
    wire = Wire(send_sems, recv_sems)
    local = {}

    def keep(key, src, dst):
        copy = pltpu.make_async_copy(src, dst, copy_sems.at[len(local)])
        copy.start()
        local[key] = copy

    partners = [dev(0, dz, dc) for dz in (1, 2, 3) for dc in (0, 1)]
    partners += [dev(1, 0, 0), dev(2, 0, 0), dev(3, 0, 0), here, before, after]
    greet(partners)
    keep("w_down", w_down_ref, w_down)
    keep("w_gate", w_gate_ref, w_gate)
    keep("w_up", w_up_ref, w_up)
    core = (c, 1 - c)

    lane = lax.broadcasted_iota(jnp.int32, (EXPERTS, 2 * tokens), 1)
    hit = lane * 0 + jnp.concatenate([route_ref[0:1, :], route_ref[1:2, :]], axis=1)
    hit = hit == lax.broadcasted_iota(jnp.int32, (EXPERTS, 2 * tokens), 0)

    def routes():
        earlier = lax.broadcasted_iota(jnp.int32, (2 * tokens, 2 * tokens), 0) % tokens
        later = lax.broadcasted_iota(jnp.int32, (2 * tokens, 2 * tokens), 1) % tokens
        upto = jnp.where(earlier <= later, 1.0, 0.0).astype(bf16)
        ones = jnp.where(hit, 1.0, 0.0).astype(bf16)
        rank = jnp.dot(ones, upto, preferred_element_type=f32) - 1.0
        return jnp.where(hit, rank, -1.0)

    rank = routes()

    def meta_own():
        gates = gate_ref[...].astype(f32)
        gates = jnp.concatenate([gates[0:1, :], gates[1:2, :]], axis=1)
        gates = jnp.where(hit, jnp.broadcast_to(gates, hit.shape), 0.0)
        either = jnp.maximum(rank, pltpu.roll(rank, tokens, 1))
        own_meta[0:EXPERTS, :] = jnp.where(lane < tokens, either, -1.0)
        own_meta[EXPERTS:, :] = gates + pltpu.roll(gates, tokens, 1)

    def slots_fill():
        slot = lax.broadcasted_iota(jnp.int32, (cap, 2 * tokens), 0).astype(f32)
        picks = [
            jnp.where(slot == rank[e : e + 1, :], 1.0, 0.0) for e in range(EXPERTS)
        ]
        pick = jnp.concatenate(picks, axis=0).astype(bf16)
        side = 4 * hid
        for low in (0, side):
            j = low // side
            taken = jnp.dot(
                pick,
                jnp.concatenate([saved_ref[:, k, j, :] for k in (0, 1)], axis=0),
                preferred_element_type=f32,
            )
            for e in range(EXPERTS):
                for m in range(4):
                    piece = taken[e * cap : (e + 1) * cap, m * hid : (m + 1) * hid]
                    at = 0 if low == 0 else hid
                    slots[e // 2, 2 * (e % 2) + m // 2, m % 2, :, at : at + hid] = piece.astype(bf16)

    def slots_start():
        for dz in (1, 3, 2):
            for dc in (0, 1):
                wire.send(
                    slots.at[:, lax.rem(z + dz, 4), core[dc]],
                    held.at[dc, 4 - dz],
                    ("held", dc, 4 - dz),
                    dev(0, dz, dc),
                )
        wire.send(slots.at[:, z, core[1]], held.at[1, 0], ("held", 1, 0), here)
        keep("slots", slots.at[:, z, c], held.at[0, 0])

    def slots_x(dc, dz):
        if (dc, dz) == (0, 0):
            local["slots"].wait()
        else:
            wire.arrive(held.at[dc, dz], ("held", dc, dz), here)
        for dx in (2, 1, 3):
            wire.send(
                held.at[dc, dz, lax.rem(x + dx, 4)],
                acts.at[dc, 4 - dx, dz],
                ("acts", dc, dz, dx),
                dev(dx, 0, 0),
            )

    def view(q):
        if q < 0:
            return own_meta, lambda dc, dx, *dz: meta.at[(dc, dx) + dz]
        return up_ref.at[q], lambda dc, dx, *dz: up.at[(q, dc, dx) + dz]

    def pair(q):
        return (1, 3) if q % 2 == 0 else (3, 1)

    def stage_a(q):
        mine, at = view(q)
        wire.send(mine, at(0, 0, 3), ("z", q, 3), dev(0, 1, 0))
        wire.send(mine, at(0, 0, 1), ("z", q, 1), dev(0, 3, 0))
        wire.send(mine, at(0, 3, 0), ("x", q, 3, 0), dev(1, 0, 0))
        wire.send(mine, at(0, 1, 0), ("x", q, 1, 0), dev(3, 0, 0))
        keep(q, mine, at(0, 0, 0))

    def along_x(q, dz):
        _, at = view(q)
        wire.send(at(0, 0, dz), at(0, 3, dz), ("x", q, 3, dz), dev(1, 0, 0))
        wire.send(at(0, 0, dz), at(0, 1, dz), ("x", q, 1, dz), dev(3, 0, 0))

    def stage_b(q, near):
        _, at = view(q)
        wire.arrive(at(0, 0, near), ("z", q, near), here)
        if near == pair(q)[0]:
            wire.send(at(0, 0, near), at(0, 0, 2), ("z", q, 2), dev(0, 4 - near, 0))
        along_x(q, near)

    def stage_c(q):
        _, at = view(q)
        wire.arrive(at(0, 0, 2), ("z", q, 2), here)
        along_x(q, 2)
        local[q].wait()
        wire.send(at(0, 0), at(1, 0), ("c", q, 0), here)

    def stage_d(q, dz):
        _, at = view(q)
        near = pair(q)[0]
        wire.arrive(at(0, near, dz), ("x", q, near, dz), here)
        wire.send(at(0, near, dz), at(0, 2, dz), ("x", q, 2, dz), dev(4 - near, 0, 0))

    def stage_h(q):
        _, at = view(q)
        plain = pair(q)[1]
        for dz in range(4):
            wire.arrive(at(0, plain, dz), ("x", q, plain, dz), here)
        wire.send(at(0, plain), at(1, plain), ("c", q, plain), here)

    def stage_i(q):
        _, at = view(q)
        near = pair(q)[0]
        wire.send(at(0, near), at(1, near), ("c", q, near), here)

    def stage_e(q):
        _, at = view(q)
        for dz in range(4):
            wire.arrive(at(0, 2, dz), ("x", q, 2, dz), here)
        wire.send(at(0, 2), at(1, 2), ("c", q, 2), here)

    def stage_f(q):
        _, at = view(q)
        for dx in range(4):
            wire.arrive(at(1, dx), ("c", q, dx), here)

    expert = me // 4
    first = (((0,), (0,)), ((), ()))

    def spread(dc, dz):
        for dx in (1, 3, 2):
            wire.arrive(acts.at[dc, 4 - dx, dz], ("acts", dc, dz, dx), here)
        for dx in range(4):
            act = held[dc, dz, x] if dx == 0 else acts[dc, dx, dz]
            slot = lax.broadcasted_iota(jnp.int32, (cap, 128), 0).astype(f32)
            hit = slot == meta[dc, dx, dz, pl.ds(expert, 1), :]
            gate = meta[dc, dx, dz, pl.ds(expert + EXPERTS, 1), :]
            pick = jnp.where(hit, 1.0, 0.0).astype(bf16)
            gate_pick = jnp.where(hit, gate, 0.0).astype(bf16)
            both = lax.dot_general(pick, act, first, preferred_element_type=f32)
            g = lax.dot_general(
                gate_pick, jnp.ones((cap, hid), bf16), first, preferred_element_type=f32
            )[:tokens]
            a = both[:tokens, :hid]
            b = both[:tokens, hid:]
            sig = jax.nn.sigmoid(a)
            silu = g * (a * sig)
            slope = g * b * sig * (1.0 + a * (1.0 - sig))
            third = (silu * b).astype(bf16)
            low = (dx * 4 + dz) * rows
            for q in range(chunks):
                mine = slice(q * rows, (q + 1) * rows)
                coef_a[q, dc, low : low + rows, :] = slope[mine]
                coef_b[q, dc, low : low + rows, :] = silu[mine]
                scaled[q, dc, low : low + rows, :] = third[mine]

    last = (((1,), (1,)), ((), ()))
    plainly = (((1,), (0,)), ((), ()))
    step = 256

    half = width // 2

    def stage_g(q, dc, h):
        if h == 0:
            mine = up[q, dc].reshape(16 * rows, width)
            grad_h = lax.dot_general(mine, w_down[...], last, preferred_element_type=f32)
            grad_a[q, dc] = (grad_h * coef_a[q, dc]).astype(bf16)
            grad_b[q, dc] = (grad_h * coef_b[q, dc]).astype(bf16)

        def body(n, carry):
            cols = pl.ds(pl.multiple_of(h * half + n * step, step), step)
            total = lax.dot_general(
                grad_a[q, dc], w_gate[:, cols], plainly, preferred_element_type=f32
            ) + lax.dot_general(grad_b[q, dc], w_up[:, cols], plainly, preferred_element_type=f32)
            part[q, dc, :, :, :, cols] = total.astype(bf16).reshape(4, 4, rows, step)
            return carry

        lax.fori_loop(0, half // step, body, 0)
        if dc == 1:
            cols = pl.ds(h * half, half)
            wire.send(
                part.at[q, 1, :, :, :, cols],
                from_core.at[q, :, :, :, cols],
                ("back c", q, h),
                here,
            )

    def weight_grad(n):
        wide = width // 4
        cols = pl.ds(n * wide, wide)
        down[:, cols] = lax.dot_general(
            scaled[...].reshape(32 * chunks * rows, hid),
            up[:, :, :, :, :, cols].reshape(32 * chunks * rows, wide),
            (((0,), (0,)), ((), ())),
            preferred_element_type=f32,
        ).astype(bf16)
        if n == 3:
            keep("down", down, down_ref)

    def half_of(ref, h):
        return ref.at[:, pl.ds(h * half, half)]

    def give_x(q, dx, dz, key, way, h):
        wire.send(
            half_of(from_core.at[q, dx, dz], h),
            half_of(from_x.at[q, key, dz], h),
            ("back x", q, key, dz, h),
            dev(way, 0, 0),
        )

    def give_z(q, dz, key, way, h):
        wire.send(
            half_of(from_core.at[q, 0, dz], h),
            half_of(from_z.at[q, key], h),
            ("back z", q, key, h),
            dev(0, way, 0),
        )

    def back_b(q, dz, h):
        by_way, plain = pair(q)
        if dz == 2:
            cols = pl.ds(h * half, half)
            wire.arrive(from_core.at[q, :, :, :, cols], ("back c", q, h), here)

        def body(dx, carry):
            mine = from_core.at[q, dx, dz]
            add_block(mine, [mine, part.at[q, 0, dx, dz]], h * half, half)
            return carry

        lax.fori_loop(0, 4, body, 0)
        give_x(q, 2, dz, 2, by_way, h)
        give_x(q, plain, dz, 4 - plain, plain, h)

    def back_c(q, dz, h):
        by_way, _ = pair(q)
        mine = from_core.at[q, by_way, dz]
        wire.arrive(half_of(from_x.at[q, 2, dz], h), ("back x", q, 2, dz, h), here)
        add_block(mine, [mine, from_x.at[q, 2, dz]], h * half, half)
        give_x(q, by_way, dz, 4 - by_way, by_way, h)

    def back_d(q, dz, h):
        by_way, plain = pair(q)
        mine = from_core.at[q, 0, dz]
        for dx in (1, 3):
            wire.arrive(half_of(from_x.at[q, dx, dz], h), ("back x", q, dx, dz, h), here)
        add_block(mine, [mine, from_x.at[q, 1, dz], from_x.at[q, 3, dz]], h * half, half)
        if dz == 2:
            give_z(q, 2, 2, by_way, h)
        if dz == plain:
            give_z(q, plain, 4 - plain, plain, h)

    def back_e(q, h):
        by_way, _ = pair(q)
        mine = from_core.at[q, 0, by_way]
        wire.arrive(half_of(from_z.at[q, 2], h), ("back z", q, 2, h), here)
        add_block(mine, [mine, from_z.at[q, 2]], h * half, half)
        give_z(q, by_way, 4 - by_way, by_way, h)

    def back_f(q, h):
        mine = from_core.at[q, 0, 0]
        for dz in (1, 3):
            wire.arrive(half_of(from_z.at[q, dz], h), ("back z", q, dz, h), here)
        add_block(mine, [mine, from_z.at[q, 1], from_z.at[q, 3]], h * half, half)
        wire.send(half_of(mine, h), half_of(landed.at[q], h), ("s", q, h), before)

    def meta_near():
        stage_b(-1, 1)
        stage_b(-1, 3)

    def meta_rest():
        stage_c(-1)
        for dz in range(4):
            stage_d(-1, dz)
        stage_h(-1)
        stage_i(-1)
        stage_e(-1)
        stage_f(-1)
        for key in ("w_down", "w_gate", "w_up"):
            local[key].wait()

    def theirs(q, h):
        stage_g(q, 1, h)

    def ours(q, h):
        stage_g(q, 0, h)

    meta_own()
    slots_fill()
    pl.semaphore_wait(pltpu.get_barrier_semaphore(), len(partners))
    stage_a(-1)
    steps = (
        (stage_a, 0), (meta_near,), (slots_start,), (slots_x, 0, 0), (slots_x, 1, 0),
        (stage_d, 0, 0), (stage_b, 0, 1), (stage_a, 1), (stage_a, 2), (stage_b, 0, 3),
        (stage_d, 0, 1), (stage_d, 1, 0), (slots_x, 0, 3), (stage_d, 2, 0), (slots_x, 0, 1),
        (stage_d, 0, 3), (slots_x, 1, 1), (slots_x, 1, 3), (meta_rest,), (spread, 0, 3),
        (spread, 0, 1), (spread, 1, 0), (spread, 1, 1), (spread, 1, 3), (spread, 0, 0),
        (slots_x, 1, 2), (slots_x, 0, 2), (spread, 1, 2), (spread, 0, 2), (stage_b, 1, 3),
        (stage_c, 0), (stage_a, 3), (stage_d, 1, 3), (stage_h, 0), (stage_d, 0, 2),
        (stage_i, 0), (stage_b, 1, 1), (stage_b, 2, 3), (stage_d, 3, 0), (stage_e, 0),
        (stage_d, 1, 1), (stage_f, 0), (theirs, 0, 0), (stage_c, 1), (stage_b, 2, 1),
        (theirs, 0, 1), (ours, 0, 0), (back_b, 0, 2, 0), (back_b, 0, 3, 0), (back_b, 0, 1, 0),
        (back_b, 0, 0, 0), (stage_d, 2, 3), (ours, 0, 1), (stage_d, 1, 2), (back_b, 0, 2, 1),
        (stage_i, 1), (stage_h, 1), (back_b, 0, 3, 1), (back_b, 0, 1, 1), (stage_b, 3, 1),
        (stage_d, 2, 1), (stage_b, 3, 3), (back_b, 0, 0, 1), (back_c, 0, 2, 0), (back_c, 0, 3, 0),
        (back_c, 0, 1, 0), (back_c, 0, 0, 0), (stage_e, 1), (back_c, 0, 2, 1), (back_c, 0, 3, 1),
        (stage_c, 2), (stage_f, 1), (theirs, 1, 0), (theirs, 1, 1), (ours, 1, 0),
        (stage_d, 3, 1), (stage_d, 3, 3), (back_c, 0, 1, 1), (back_b, 1, 2, 0), (back_c, 0, 0, 1),
        (ours, 1, 1), (back_d, 0, 2, 0), (back_b, 1, 1, 0), (stage_c, 3), (back_b, 1, 2, 1),
        (back_b, 1, 1, 1), (back_d, 0, 3, 0), (back_b, 1, 3, 0), (back_b, 1, 0, 0), (back_b, 1, 3, 1),
        (back_b, 1, 0, 1), (stage_d, 2, 2), (stage_i, 2), (back_d, 0, 0, 0), (back_d, 0, 1, 0),
        (back_c, 1, 2, 0), (back_d, 0, 2, 1), (back_c, 1, 1, 0), (back_d, 0, 3, 1), (stage_h, 3),
        (stage_h, 2), (back_c, 1, 2, 1), (back_c, 1, 1, 1), (back_c, 1, 3, 0), (back_e, 0, 0),
        (back_c, 1, 0, 0), (back_c, 1, 3, 1), (back_d, 0, 1, 1), (back_c, 1, 0, 1), (back_d, 0, 0, 1),
        (back_e, 0, 1), (stage_e, 2), (back_d, 1, 2, 0), (back_d, 1, 1, 0), (stage_d, 3, 2),
        (stage_i, 3), (stage_f, 2), (theirs, 2, 0), (back_d, 1, 1, 1), (back_d, 1, 2, 1),
        (theirs, 2, 1), (ours, 2, 0), (back_f, 0, 0), (back_b, 2, 2, 0), (back_d, 1, 3, 1),
        (back_d, 1, 0, 1), (back_d, 1, 3, 0), (back_d, 1, 0, 0), (back_b, 2, 3, 0), (back_b, 2, 1, 0),
        (back_b, 2, 0, 0), (ours, 2, 1), (stage_e, 3), (back_b, 2, 2, 1), (back_f, 0, 1),
        (back_b, 2, 3, 1), (back_e, 1, 0), (back_b, 2, 1, 1), (back_c, 2, 2, 0), (back_b, 2, 0, 1),
        (back_c, 2, 3, 0), (stage_f, 3), (theirs, 3, 0), (back_c, 2, 1, 0), (back_c, 2, 0, 0),
        (back_e, 1, 1), (theirs, 3, 1), (back_c, 2, 2, 1), (ours, 3, 0), (back_c, 2, 3, 1),
        (back_b, 3, 2, 0), (back_d, 2, 2, 0), (back_b, 3, 1, 0), (ours, 3, 1), (back_b, 3, 2, 1),
        (back_b, 3, 1, 1), (back_c, 2, 0, 1), (back_c, 2, 1, 1), (back_d, 2, 3, 0), (back_b, 3, 3, 0),
        (back_b, 3, 0, 0), (back_d, 2, 1, 0), (back_f, 1, 0), (weight_grad, 0), (back_c, 3, 2, 0),
        (back_c, 3, 1, 0), (back_d, 2, 0, 0), (back_d, 2, 2, 1), (back_b, 3, 3, 1), (back_b, 3, 0, 1),
        (back_d, 2, 3, 1), (back_c, 3, 2, 1), (weight_grad, 1), (back_c, 3, 1, 1), (back_f, 1, 1),
        (back_c, 3, 3, 0), (weight_grad, 2), (weight_grad, 3), (back_d, 3, 2, 0), (back_e, 2, 0),
        (back_d, 2, 0, 1), (back_d, 3, 1, 0), (back_c, 3, 0, 0), (back_c, 3, 3, 1), (back_d, 2, 1, 1),
        (back_c, 3, 0, 1), (back_d, 3, 2, 1), (back_d, 3, 1, 1), (back_e, 2, 1), (back_d, 3, 3, 0),
        (back_d, 3, 0, 0), (back_d, 3, 3, 1), (back_d, 3, 0, 1), (back_e, 3, 0), (back_f, 2, 0),
        (back_e, 3, 1), (back_f, 3, 0), (back_f, 2, 1), (back_f, 3, 1),
    )
    for stage, *at in steps:
        stage(*at)
    for q in range(chunks):
        for h in (0, 1):
            wire.arrive(half_of(landed.at[q], h), ("s", q, h), here)
        keep(("out", q), landed.at[q], out_ref.at[q])
    local["down"].wait()
    for q in range(chunks):
        local["out", q].wait()
    wire.drain()


def store_kernel(grad_in_ref, grad_down_ref, out_ref, down_ref):
    out_ref[...] = grad_in_ref[...]
    down_ref[...] = grad_down_ref[...]


def on_device(grad_out, pre_act, route_ids, route_gate, w_gate, w_up, w_down):
    tokens = grad_out.shape[1]
    width = grad_out.shape[2]
    hid = w_down.shape[1]
    cap = 3 * tokens // 8
    chunks = tokens // ROWS
    bf16 = jnp.bfloat16
    f32 = jnp.float32
    saved = pre_act[0]
    up = grad_out[0].reshape(chunks, ROWS, width)

    vm = pl.BlockSpec(memory_space=VMEM)
    anywhere = pl.BlockSpec(memory_space=pl.ANY)
    dma = pltpu.SemaphoreType.DMA
    block = (ROWS, width)
    copies = 31 + 19 * (chunks + 1) + 34 * chunks
    grad_in, grad_down = pl.pallas_call(
        layer_kernel,
        out_shape=(
            jax.ShapeDtypeStruct((chunks,) + block, bf16),
            jax.ShapeDtypeStruct((hid, width), bf16),
        ),
        in_specs=[vm] * 4 + [anywhere] * 3,
        out_specs=(anywhere, anywhere),
        scratch_shapes=[
            VMEM((chunks, 2, 4, 4) + block, bf16),
            VMEM((2, 4, 4, 2 * EXPERTS, 128), f32),
            VMEM((2 * EXPERTS, 128), f32),
            VMEM((4, 4, 2, cap, 2 * hid), bf16),
            VMEM((2, 4, 4, cap, 2 * hid), bf16),
            VMEM((2, 4, 4, cap, 2 * hid), bf16),
            VMEM((hid, width), bf16),
            VMEM((hid, width), bf16),
            VMEM((hid, width), bf16),
            VMEM((chunks, 2, 16 * ROWS, hid), f32),
            VMEM((chunks, 2, 16 * ROWS, hid), f32),
            VMEM((chunks, 2, 16 * ROWS, hid), bf16),
            VMEM((chunks, 2, 16 * ROWS, hid), bf16),
            VMEM((chunks, 2, 16 * ROWS, hid), bf16),
            VMEM((hid, width), bf16),
            VMEM((chunks, 2, 4, 4) + block, bf16),
            VMEM((chunks, 4, 4) + block, bf16),
            VMEM((chunks, 4, 4) + block, bf16),
            VMEM((chunks, 4) + block, bf16),
            VMEM((chunks,) + block, bf16),
            dma((copies,)),
            dma((copies,)),
            dma((2 * chunks + 6,)),
        ],
        compiler_params=pltpu.CompilerParams(
            collective_id=0, has_side_effects=True, vmem_limit_bytes=60 << 20
        ),
        name="layer",
    )(up, saved, route_ids[0].T, route_gate[0].T, w_gate[0].T, w_up[0].T, w_down[0])
    grad_in = grad_in.reshape(tokens, width)
    return tuple(
        out[None]
        for out in pl.pallas_call(
            store_kernel,
            out_shape=(
                jax.ShapeDtypeStruct(grad_in.shape, bf16),
                jax.ShapeDtypeStruct(grad_down.shape, bf16),
            ),
            in_specs=[vm] * 2,
            out_specs=(vm, vm),
            name="store",
        )(grad_in, grad_down)
    )


def solution(mesh):
    tok = P("section", "expert", None)
    return jax.shard_map(
        on_device,
        mesh=mesh,
        in_specs=(
            tok,
            P("section", "expert", None, None, None),
            tok,
            tok,
            P("section", None, "expert"),
            P("section", None, "expert"),
            tok,
        ),
        out_specs=(tok, tok),
        check_vma=False,
    )
```
